256 devices in a mesh: seq: 64 (over y, z_hi, x), head: 4 (over z_lo, core).
Axes of the slice: x: 4, y: 4, z: 8 (z_hi: 4, z_lo: 2; z = z_hi * 2 + z_lo), core: 2. Of those that a mesh axis runs over, the one named last changes fastest.
Arguments:
- queries: bfloat16 [16384, 3072], P('seq', 'head'), may hold values from -6 to 6
- keys: bfloat16 [16384, 3072], P('seq', 'head'), may hold values from -6 to 6
- values: bfloat16 [16384, 3072], P('seq', 'head'), may hold values from -6 to 6
- grad_out: bfloat16 [16384, 3072], P('seq', 'head'), may hold values from -6 to 6
- scene_keys: bfloat16 [256, 3072], P(('seq', 'head')), may hold values from -6 to 6
- scene_values: bfloat16 [256, 3072], P(('seq', 'head')), may hold values from -6 to 6
- valid: int32 [256], replicated, may hold values from 2 to 64
- pattern: int32 [256, 3], replicated, may hold values from 0 to 255, as said below
Outputs:
- attended: bfloat16 [16384, 3072], P('seq', 'head')
- grad_queries: bfloat16 [16384, 3072], P('seq', 'head')
- grad_keys: bfloat16 [16384, 3072], P('seq', 'head')
- grad_values: bfloat16 [16384, 3072], P('seq', 'head')
- grad_scene_keys: bfloat16 [256, 3072], P(('seq', 'head'))
- grad_scene_values: bfloat16 [256, 3072], P(('seq', 'head'))
The draws below stay inside these ranges and needn't reach their ends.
Inputs may be any that keep to these rules, and one draw needn't show every extreme that they name: `pattern`: the 12 entries of the query blocks of one seq index all name blocks of other seq indices; no seq index supplies more than 1 of them to one seq index, and to each seq index some seq index supplies exactly 1.
All inputs are finite; a program needn't handle non-finite values.
Results may differ from the reference program's by a relative error of at most 0.0061.
Values may be sent and summed in bfloat16 or wider, within the bound.
No kernel may reach another device: no remote copies, remote signals or barrier semaphores. Data moves between devices by JAX's collectives and lax.ppermute only.
A program may use at most 128 MiB of HBM per device.

```python
import jax
import jax.numpy as jnp
from jax import lax

HEADS = 24
DH = 128
BLK = 64
RAND = 3
BLK_DEV = 4
FEAT = 3072
NBLK = 256
TOKENS = 16384
SCENE = 256
N_HEAD = 4


def draw_queries(key, part):
    sample_key = jax.random.fold_in(key, 11)
    sample = jnp.clip(jax.random.normal(sample_key, (NBLK, BLK, FEAT), jnp.float32), -6.0, 6.0)
    return sample.reshape(TOKENS, FEAT).astype(jnp.bfloat16)


def draw_keys(key, part):
    sample_key = jax.random.fold_in(key, 12)
    sample = jnp.clip(jax.random.normal(sample_key, (NBLK, BLK, FEAT), jnp.float32), -6.0, 6.0)
    return sample.reshape(TOKENS, FEAT).astype(jnp.bfloat16)


def draw_pattern(key, part):
    seq_count = NBLK // BLK_DEV
    requests = BLK_DEV * RAND
    keys_first = jax.random.split(jax.random.fold_in(key, 5), seq_count)
    keys_second = jax.random.split(jax.random.fold_in(key, 6), seq_count)
    perms = jax.vmap(lambda subkey: jax.random.permutation(subkey, seq_count - 1))(keys_first)
    orders = jax.vmap(lambda subkey: jax.random.permutation(subkey, requests))(keys_second)
    column = jnp.arange(requests, dtype=jnp.int32) % (seq_count - 1)
    offset = perms[:, column] + 1
    offset = jnp.take_along_axis(offset, orders, axis=1)
    device = (jnp.arange(seq_count, dtype=jnp.int32)[:, None] + offset) % seq_count
    block = jax.random.randint(jax.random.fold_in(key, 7), (seq_count, requests), 0, BLK_DEV)
    return (device * BLK_DEV + block).reshape(NBLK, RAND).astype(jnp.int32)


def with_ends(entries, own_key, least, top_value):
    longest = entries.shape.index(max(entries.shape))
    spots = []
    for shift in (0, 1):
        where = [jax.random.randint(jax.random.fold_in(own_key, axis), (), 0, length) for axis, length in enumerate(entries.shape)]
        where[longest] = (where[longest] + shift) % entries.shape[longest]
        spots.append(tuple(where))
    return entries.at[spots[0]].set(least).at[spots[1]].set(top_value)


def shard_levels(stream_key, dims, pieces, least, largest):
    def one(position, parts):
        draws = jax.random.uniform(jax.random.fold_in(jax.random.fold_in(stream_key, 6), position), (parts,), jnp.float32, least / len(pieces), largest / len(pieces))
        return jnp.repeat(jnp.exp(draws), dims[position] // parts).reshape((-1,) + (1,) * (len(dims) - position - 1))

    loudness = one(*pieces[0])
    for cut in pieces[1:]:
        loudness = loudness * one(*cut)
    return loudness


def normal_values(stream_key, extent, scale, reach, shards=(), kind=jnp.bfloat16):
    values = scale * jax.random.normal(stream_key, extent, jnp.float32)
    if shards:
        values = values * shard_levels(stream_key, extent, shards, -0.22, 0.18)
    return jnp.clip(values, -reach, reach).astype(kind)


def setup_inputs(seed: int = 0) -> dict:
    key_list = jax.random.split(jax.random.key(seed), 9)
    return {
        "queries": draw_queries(jax.random.fold_in(key_list[8], 71), 0),
        "keys": draw_keys(jax.random.fold_in(key_list[8], 71), 0),
        "values": normal_values(key_list[2], (TOKENS, FEAT), 1.0, 6.0, ((0, 64), (1, 4))),
        "grad_out": normal_values(key_list[3], (TOKENS, FEAT), 1.0, 6.0, ((0, 64), (1, 4))),
        "scene_keys": normal_values(key_list[4], (SCENE, FEAT), 1.0, 6.0, ((0, 256),)),
        "scene_values": normal_values(key_list[5], (SCENE, FEAT), 1.0, 6.0, ((0, 256),)),
        "valid": with_ends(jax.random.randint(key_list[6], (NBLK,), 2, BLK + 1), jax.random.fold_in(key_list[6], 1), 2, BLK).astype(jnp.int32),
        "pattern": draw_pattern(jax.random.fold_in(key_list[8], 71), 0),
    }


def rounded(value):
    return lax.optimization_barrier(value.astype(jnp.bfloat16)).astype(jnp.float32)


def block_terms(query, near_keys, near_values, scene_k, scene_v, key_live, query_live, grad_out):
    scale = DH ** -0.5
    near_scores = jnp.einsum('gqhd,gkhd->ghqk', query, near_keys) * scale
    near_scores = jnp.where(key_live[:, None, None, :], near_scores, -1e30)
    scene_scores = jnp.einsum('gqhd,khd->ghqk', query, scene_k) * scale
    highest = jnp.maximum(jnp.max(near_scores, axis=3, keepdims=True), jnp.max(scene_scores, axis=3, keepdims=True))
    near_exp = jnp.exp(near_scores - highest)
    scene_exp = jnp.exp(scene_scores - highest)
    denominator = jnp.sum(near_exp, axis=3, keepdims=True) + jnp.sum(scene_exp, axis=3, keepdims=True)
    near_prob = near_exp / denominator
    scene_prob = scene_exp / denominator
    near_round = rounded(near_prob)
    scene_round = rounded(scene_prob)
    live_rows = query_live[:, :, None, None]
    attended = jnp.einsum('ghqk,gkhd->gqhd', near_round, near_values) + jnp.einsum('ghqk,khd->gqhd', scene_round, scene_v)
    attended = jnp.where(live_rows, attended, 0.0).astype(jnp.bfloat16)
    grad_live = jnp.where(live_rows, grad_out, 0.0)
    near_dprob = jnp.einsum('gqhd,gkhd->ghqk', grad_live, near_values)
    scene_dprob = jnp.einsum('gqhd,khd->ghqk', grad_live, scene_v)
    delta = jnp.sum(near_prob * near_dprob, axis=3, keepdims=True) + jnp.sum(scene_prob * scene_dprob, axis=3, keepdims=True)
    near_dscore = rounded(near_prob * (near_dprob - delta) * scale)
    scene_dscore = rounded(scene_prob * (scene_dprob - delta) * scale)
    grad_query = jnp.einsum('ghqk,gkhd->gqhd', near_dscore, near_keys) + jnp.einsum('ghqk,khd->gqhd', scene_dscore, scene_k)
    grad_near_k = jnp.einsum('ghqk,gqhd->gkhd', near_dscore, query)
    grad_near_v = jnp.einsum('ghqk,gqhd->gkhd', near_round, grad_live)
    grad_scene_k = jnp.einsum('ghqk,gqhd->khd', scene_dscore, query)
    grad_scene_v = jnp.einsum('ghqk,gqhd->khd', scene_round, grad_live)
    return attended, grad_query.astype(jnp.bfloat16), grad_near_k, grad_near_v, grad_scene_k, grad_scene_v


def add_near(total, terms, first_block, group_size):
    window_acc = lax.dynamic_slice_in_dim(total, first_block, group_size + 2, 0)
    window_acc = window_acc.at[0:group_size].add(terms[:, 0])
    window_acc = window_acc.at[1:group_size + 1].add(terms[:, 1])
    window_acc = window_acc.at[2:].add(terms[:, 2])
    return lax.dynamic_update_slice_in_dim(total, window_acc, first_block, 0)


def reference(queries, keys, values, grad_out, scene_keys, scene_values, valid, pattern):
    head_count = HEADS // N_HEAD
    features = head_count * DH
    group_size = min(8, BLK_DEV)
    offsets = jnp.arange(BLK, dtype=jnp.int32)
    padded_valid = jnp.concatenate([jnp.zeros((1,), jnp.int32), valid.astype(jnp.int32), jnp.zeros((1,), jnp.int32)])
    attended_list, gquery_list, gkey_list, gvalue_list, gscene_k_list, gscene_v_list = [], [], [], [], [], []
    for part_index in range(N_HEAD):
        column_low = part_index * features

        def columns(array):
            return array[:, column_low:column_low + features].astype(jnp.float32)

        query_all = columns(queries).reshape(NBLK, BLK, head_count, DH)
        key_all = columns(keys).reshape(NBLK, BLK, head_count, DH)
        value_all = columns(values).reshape(NBLK, BLK, head_count, DH)
        grad_all = columns(grad_out).reshape(NBLK, BLK, head_count, DH)
        key_pad = jnp.pad(key_all, ((1, 1), (0, 0), (0, 0), (0, 0)))
        value_pad = jnp.pad(value_all, ((1, 1), (0, 0), (0, 0), (0, 0)))
        scene_k = columns(scene_keys).reshape(SCENE, head_count, DH)
        scene_v = columns(scene_values).reshape(SCENE, head_count, DH)

        def advance(running, group_index):
            key_acc, value_acc, scene_k_acc, scene_v_acc = running
            first_block = group_index.astype(jnp.int32) * group_size
            query_grp = lax.dynamic_slice_in_dim(query_all, first_block, group_size, 0)
            grad_grp = lax.dynamic_slice_in_dim(grad_all, first_block, group_size, 0)
            window_k = lax.dynamic_slice_in_dim(key_pad, first_block, group_size + 2, 0)
            window_v = lax.dynamic_slice_in_dim(value_pad, first_block, group_size + 2, 0)
            random_ids = lax.dynamic_slice_in_dim(pattern, first_block, group_size, 0).astype(jnp.int32)
            near_k = jnp.concatenate([window_k[0:group_size, None], window_k[1:group_size + 1, None], window_k[2:, None], key_all[random_ids]], axis=1)
            near_v = jnp.concatenate([window_v[0:group_size, None], window_v[1:group_size + 1, None], window_v[2:, None], value_all[random_ids]], axis=1)
            near_k = near_k.reshape(group_size, (3 + RAND) * BLK, head_count, DH)
            near_v = near_v.reshape(group_size, (3 + RAND) * BLK, head_count, DH)
            window_count = lax.dynamic_slice_in_dim(padded_valid, first_block, group_size + 2, 0)
            counts = jnp.concatenate([window_count[0:group_size, None], window_count[1:group_size + 1, None], window_count[2:, None], valid[random_ids]], axis=1)
            key_live = (offsets[None, None, :] < counts[:, :, None]).reshape(group_size, (3 + RAND) * BLK)
            query_live = offsets[None, :] < lax.dynamic_slice_in_dim(valid, first_block, group_size, 0)[:, None]
            attended, grad_query, grad_k, grad_v, grad_sk, grad_sv = block_terms(query_grp, near_k, near_v, scene_k, scene_v, key_live, query_live, grad_grp)
            grad_k = grad_k.reshape(group_size, 3 + RAND, BLK, head_count, DH)
            grad_v = grad_v.reshape(group_size, 3 + RAND, BLK, head_count, DH)
            key_acc = add_near(key_acc, grad_k, first_block, group_size)
            value_acc = add_near(value_acc, grad_v, first_block, group_size)
            targets = random_ids.reshape(-1) + 1
            key_acc = key_acc.at[targets].add(rounded(grad_k[:, 3:]).reshape(group_size * RAND, BLK, head_count, DH))
            value_acc = value_acc.at[targets].add(rounded(grad_v[:, 3:]).reshape(group_size * RAND, BLK, head_count, DH))
            return (key_acc, value_acc, scene_k_acc + grad_sk, scene_v_acc + grad_sv), (attended, grad_query)

        initial = (jnp.zeros((NBLK + 2, BLK, head_count, DH), jnp.float32), jnp.zeros((NBLK + 2, BLK, head_count, DH), jnp.float32),
                   jnp.zeros((SCENE, head_count, DH), jnp.float32), jnp.zeros((SCENE, head_count, DH), jnp.float32))
        running, (attended_all, gquery_all) = lax.scan(advance, initial, jnp.arange(NBLK // group_size, dtype=jnp.int32))
        key_acc, value_acc, scene_k_acc, scene_v_acc = running
        attended_list.append(attended_all.reshape(TOKENS, features))
        gquery_list.append(gquery_all.reshape(TOKENS, features))
        gkey_list.append(key_acc[1:NBLK + 1].reshape(TOKENS, features).astype(jnp.bfloat16))
        gvalue_list.append(value_acc[1:NBLK + 1].reshape(TOKENS, features).astype(jnp.bfloat16))
        gscene_k_list.append(scene_k_acc.reshape(SCENE, features).astype(jnp.bfloat16))
        gscene_v_list.append(scene_v_acc.reshape(SCENE, features).astype(jnp.bfloat16))
    return (jnp.concatenate(attended_list, axis=1), jnp.concatenate(gquery_list, axis=1), jnp.concatenate(gkey_list, axis=1),
            jnp.concatenate(gvalue_list, axis=1), jnp.concatenate(gscene_k_list, axis=1), jnp.concatenate(gscene_v_list, axis=1))
```

```python
import jax
import jax.numpy as jnp
from jax import lax
from jax.experimental import pallas as pl
from jax.experimental.pallas import tpu as pltpu
from jax.sharding import PartitionSpec as P

DH = 128
BLK = 64
RAND = 3
F32 = jnp.float32
BF16 = jnp.bfloat16
LOG2E = 1.4426950408889634


def ring_shift(x, stride, size, by):
    count = lax.axis_size("seq")
    pairs = []
    for i in range(count):
        c = (i // stride) % size
        pairs.append((i, i + ((c + by) % size - c) * stride))
    return lax.ppermute(x, "seq", pairs)


def passed_along(x, by):
    length = lax.axis_size("seq")
    pairs = [(i, i + by) for i in range(length) if 0 <= i + by < length]
    return lax.ppermute(x, "seq", pairs)


def gather_axis(x, stride, size):
    return jnp.concatenate(
        [x] + [ring_shift(x, stride, size, s) for s in range(1, size)], axis=1
    )


def scatter_axis(x, stride, size):
    rows = x.shape[1] // size
    total = x[:, :rows]
    for s in range(1, size):
        total = total + ring_shift(x[:, s * rows : (s + 1) * rows], stride, size, size - s)
    return total


def nt(a, b):
    return lax.dot_general(a, b, (((1,), (1,)), ((), ())), preferred_element_type=F32)


def nn(a, b):
    return lax.dot_general(a, b, (((1,), (0,)), ((), ())), preferred_element_type=F32)


def tn(a, b):
    return lax.dot_general(a, b, (((0,), (0,)), ((), ())), preferred_element_type=F32)


def attention_kernel(
    bias, live, q, go, k, v, lo, hi, rnd, scn, att, dq, d_own, d_halo, d_rnd, d_scn
):
    tokens = q.shape[0]
    far = rnd.shape[1]
    scale = DH ** (-0.5)
    key = jnp.concatenate([lo[0], k[...], hi[0], rnd[0], scn[0]], axis=0)
    val = jnp.concatenate([lo[1], v[...], hi[1], rnd[1], scn[1]], axis=0)
    query = q[...]
    grad = go[...]
    s = nt(key, query) * (scale * LOG2E) + bias[...]
    e = jnp.exp2(s - jnp.max(s, axis=0, keepdims=True))
    p = e * (1.0 / jnp.sum(e, axis=0, keepdims=True))
    pb = p.astype(BF16)
    dp = nt(val, grad)
    delta = jnp.sum(p * dp, axis=0, keepdims=True)
    ds = (p * (dp - delta) * scale).astype(BF16)
    att[...] = (tn(val, pb) * live[...]).T.astype(BF16)
    dq[...] = tn(key, ds).T.astype(BF16)
    for which, (left, right) in enumerate(((ds, query), (pb, grad))):
        d = nn(left, right)
        d_halo[which, :BLK] = d[:BLK].astype(BF16)
        d_own[which] = d[BLK : BLK + tokens]
        d_halo[which, BLK:] = d[BLK + tokens : 2 * BLK + tokens].astype(BF16)
        d_rnd[which] = d[2 * BLK + tokens : 2 * BLK + tokens + far].astype(BF16)
        d_scn[which] = d[2 * BLK + tokens + far :]


def attention(bias, live, q, go, k, v, lo, hi, rnd, scn):
    tokens, features = q.shape
    heads = features // DH
    far = rnd.shape[1]
    scene = scn.shape[1]

    def whole(x):
        return pl.BlockSpec(x.shape, lambda h: (0,) * x.ndim)

    def flat(rows):
        return pl.BlockSpec((rows, DH), lambda h: (0, h))

    def pair(rows):
        return pl.BlockSpec((2, rows, DH), lambda h: (0, 0, h))

    def shaped(shape, dtype):
        return jax.ShapeDtypeStruct(shape, dtype)

    return pl.pallas_call(
        attention_kernel,
        grid=(heads,),
        in_specs=[whole(bias), whole(live)]
        + [flat(tokens)] * 4
        + [pair(BLK), pair(BLK), pair(far), pair(scene)],
        out_specs=[
            flat(tokens),
            flat(tokens),
            pair(tokens),
            pair(2 * BLK),
            pair(far),
            pair(scene),
        ],
        out_shape=[
            shaped((tokens, features), BF16),
            shaped((tokens, features), BF16),
            shaped((2, tokens, features), F32),
            shaped((2, 2 * BLK, features), BF16),
            shaped((2, far, features), BF16),
            shaped((2, scene, features), F32),
        ],
        compiler_params=pltpu.CompilerParams(vmem_limit_bytes=48 << 20),
        name="attention",
    )(bias, live, q, go, k, v, lo, hi, rnd, scn)


def per_device(queries, keys, values, grad_out, scene_keys, scene_values, valid, pattern):
    seq = lax.axis_size("seq")
    position = lax.axis_index("seq")
    tokens, features = queries.shape
    blocks = tokens // BLK
    requests = blocks * RAND
    half = seq // 2
    side = round(seq ** (1 / 3))
    axes = (side, side * side, 1)

    row = jnp.arange(tokens, dtype=jnp.int32)
    pair_of, rest = row // (2 * blocks), row % (2 * blocks)
    origin = (rest // 2) * BLK + pair_of * 2 + rest % 2
    spread = (origin[:, None] == row[None, :]).astype(BF16)
    stacked = jnp.stack([keys, values])
    out_1 = jnp.einsum("rs,xsf->xrf", spread, stacked, preferred_element_type=F32).astype(BF16)
    in_1 = lax.all_to_all(
        out_1.reshape(seq, 2 * blocks, features), "seq", split_axis=0, concat_axis=0, tiled=True
    )

    lo = passed_along(stacked[:, tokens - BLK :], 1)
    hi = passed_along(stacked[:, :BLK], -1)

    scene = jnp.stack([scene_keys, scene_values])
    scn = lax.all_to_all(scene, "head", split_axis=2, concat_axis=1, tiled=True)
    for stride in axes:
        scn = gather_axis(scn, stride, side)
    scene_rows = scn.shape[1]

    wanted = (pattern.reshape(-1)[:, None] * 2 + jnp.arange(2, dtype=jnp.int32)).reshape(-1)
    choose = (
        wanted[:, None] == jnp.arange(2 * blocks * seq, dtype=jnp.int32)[None, :]
    ).astype(BF16)
    out_2 = jnp.einsum(
        "rc,cf->rf",
        choose,
        in_1.reshape(2 * blocks * seq, features),
        preferred_element_type=F32,
    ).astype(BF16)
    in_2 = lax.all_to_all(
        out_2.reshape(seq, 2 * requests, features), "seq", split_axis=0, concat_axis=0, tiled=True
    )
    rnd = in_2.reshape(2, half * 2 * requests, features)
    far = half * 2 * requests

    padded = jnp.concatenate([jnp.zeros((1,), jnp.int32), valid, jnp.zeros((1,), jnp.int32)])
    near_count = lax.dynamic_slice_in_dim(padded, position * blocks, blocks + 2, 0)
    own = lax.dynamic_slice_in_dim(pattern, position * blocks, blocks, 0).reshape(requests)
    far_count = valid[own]
    query_block = row // BLK
    w = jnp.arange((blocks + 2) * BLK, dtype=jnp.int32)
    w_block = w // BLK
    near_ok = (
        ((w % BLK) < near_count[w_block])[:, None]
        & (w_block[:, None] >= query_block[None, :])
        & (w_block[:, None] <= query_block[None, :] + 2)
    )
    r = jnp.arange(far, dtype=jnp.int32)
    r_request = (r % (2 * requests)) // 2
    r_token = (r // (2 * requests)) * 2 + r % 2
    far_ok = (r_token < far_count[r_request])[:, None] & (
        (r_request // RAND)[:, None] == query_block[None, :]
    )
    ok = jnp.concatenate([near_ok, far_ok, jnp.ones((scene_rows, tokens), jnp.bool_)], axis=0)
    bias = jnp.where(ok, 0.0, -1e30).astype(F32)
    count = lax.dynamic_slice_in_dim(valid, position * blocks, blocks, 0)
    query_live = (row % BLK) < count[query_block]
    live = query_live.astype(F32)[None, :]
    grad_live = jnp.where(query_live[:, None], grad_out, jnp.zeros((), BF16))

    attended, grad_query, d_own, d_halo, d_rnd, d_scn = attention(
        bias, live, queries, grad_live, keys, values, lo, hi, rnd, scn
    )

    back_1 = lax.all_to_all(
        d_rnd.reshape(seq, 2 * requests, features), "seq", split_axis=0, concat_axis=0, tiled=True
    )
    from_right = passed_along(d_halo[:, :BLK], -1)
    from_left = passed_along(d_halo[:, BLK:], 1)
    summed = d_scn
    for stride in reversed(axes):
        summed = scatter_axis(summed, stride, side)
    scene_grad = lax.all_to_all(summed, "head", split_axis=1, concat_axis=2, tiled=True)

    held = jnp.einsum(
        "rc,rf->cf",
        choose,
        back_1.reshape(seq * 2 * requests, features),
        preferred_element_type=F32,
    ).astype(BF16)
    back_2 = lax.all_to_all(
        held.reshape(seq, 2 * blocks, features), "seq", split_axis=0, concat_axis=0, tiled=True
    )
    total = d_own + jnp.einsum(
        "rs,xrf->xsf", spread, back_2.reshape(2, tokens, features), preferred_element_type=F32
    )
    total = total.at[:, tokens - BLK :].add(from_right.astype(F32))
    total = total.at[:, :BLK].add(from_left.astype(F32))
    total = total.astype(BF16)
    scene_grad = scene_grad.astype(BF16)
    return (attended, grad_query, total[0], total[1], scene_grad[0], scene_grad[1])


def solution(mesh):
    block = P("seq", "head")
    rows = P(("seq", "head"), None)
    return jax.shard_map(
        per_device,
        mesh=mesh,
        in_specs=(block, block, block, block, rows, rows, P(), P()),
        out_specs=(block, block, block, block, rows, rows),
        check_vma=False,
    )
```

```python
import jax
import jax.numpy as jnp
from jax import lax
from jax.experimental import pallas as pl
from jax.experimental.pallas import tpu as pltpu
from jax.sharding import PartitionSpec as P

DH = 128
BLK = 64
RAND = 3
SIDE = 4
PLANE = SIDE * SIDE
TAKE = BLK // PLANE
SCENE_PAD = 8
PARTS = 2
F32 = jnp.float32
BF16 = jnp.bfloat16
LOG2E = 1.4426950408889634


def shift_z(x, by):
    pairs = []
    for i in range(lax.axis_size("seq")):
        z = i // SIDE % SIDE
        pairs.append((i, i + ((z + by) % SIDE - z) * SIDE))
    return lax.ppermute(x, "seq", pairs)


def exchange(x):
    groups = [
        [(y * SIDE + z) * SIDE + c for y in range(SIDE) for c in range(SIDE)]
        for z in range(SIDE)
    ]
    return lax.all_to_all(
        x, "seq", split_axis=0, concat_axis=0, axis_index_groups=groups, tiled=True
    )


def after(x, *others):
    return lax.optimization_barrier((x,) + others)[0]


def nt(a, b):
    return lax.dot_general(a, b, (((1,), (1,)), ((), ())), preferred_element_type=F32)


def nn(a, b):
    return lax.dot_general(a, b, (((1,), (0,)), ((), ())), preferred_element_type=F32)


def tn(a, b):
    return lax.dot_general(a, b, (((0,), (0,)), ((), ())), preferred_element_type=F32)


def holder_row(token, blocks):
    return (token % BLK) // TAKE * (TAKE * blocks) + token // BLK * TAKE + token % TAKE


def spread_kernel(k, v, *outs):
    tokens, features = k.shape
    width = features // PARTS
    r = lax.broadcasted_iota(jnp.int32, (tokens, tokens), 0)
    t = lax.broadcasted_iota(jnp.int32, (tokens, tokens), 1)
    order = (holder_row(t, tokens // BLK) == r).astype(F32).astype(BF16)
    for part, out in enumerate(outs):
        cols = slice(part * width, (part + 1) * width)
        out[:, :width] = nn(order, k[:, cols]).astype(BF16)
        out[:, width:] = nn(order, v[:, cols]).astype(BF16)


def spread(k, v):
    tokens, features = k.shape
    return pl.pallas_call(
        spread_kernel,
        out_shape=[jax.ShapeDtypeStruct((tokens, 2 * features // PARTS), BF16)] * PARTS,
        name="spread",
    )(k, v)


def plan_kernel(place, counts, pattern, bias, live, live_col, choose):
    rows, tokens = bias.shape
    blocks = tokens // BLK
    total = counts.shape[0]
    position = place[0]
    first = position * blocks
    z = position // SIDE % SIDE
    piece = choose.shape[1] // SIDE
    held = piece - SCENE_PAD
    requests = blocks * RAND + 2
    asked = requests * TAKE

    def clamp(block):
        return jnp.minimum(jnp.maximum(block, 0), total - 1)

    def request(seq_index, i):
        start = seq_index * blocks
        if i < blocks * RAND:
            return pattern[start + i // RAND, i % RAND]
        return clamp(start - 1 if i == blocks * RAND else start + blocks)

    query_block = lax.broadcasted_iota(jnp.int32, (BLK, tokens), 1) // BLK
    offset = lax.broadcasted_iota(jnp.int32, (BLK, tokens), 0)
    for b in range(blocks):
        ok = (offset < counts[first + b]) & (query_block <= b + 1) & (query_block + 1 >= b)
        bias[b * BLK : (b + 1) * BLK] = jnp.where(ok, 0.0, -1e30).astype(F32)
    per = asked + SIDE * groups_of(choose, requests)
    r = lax.broadcasted_iota(jnp.int32, (per, tokens), 0)
    column_block = lax.broadcasted_iota(jnp.int32, (per, tokens), 1) // BLK
    count = jnp.where(r >= asked, BLK, 0)
    for i in range(requests):
        c = request(position, i)
        live_keys = counts[c]
        if i < blocks * RAND:
            column = i // RAND
        elif i == blocks * RAND:
            column = 0
            live_keys = jnp.where(first > 0, live_keys, 0)
        else:
            column = blocks - 1
            live_keys = jnp.where(first + blocks < total, live_keys, 0)
        here = (r // TAKE == i) & (column_block == column)
        count = jnp.where(here, live_keys, count)
    slot_token = jnp.where(r >= asked, 0, r % TAKE)
    for g in range(PLANE):
        ok = slot_token + jnp.where(r >= asked, 0, g * TAKE) < count
        bias[tokens + g * per : tokens + (g + 1) * per] = jnp.where(ok, 0.0, -1e30).astype(F32)
    lane = lax.broadcasted_iota(jnp.int32, (8, tokens), 1)
    bound = jnp.zeros((8, tokens), jnp.int32)
    row = lax.broadcasted_iota(jnp.int32, (BLK, DH), 0)
    for b in range(blocks):
        bound = jnp.where(lane // BLK == b, counts[first + b], bound)
        live_col[b * BLK : (b + 1) * BLK] = (row < counts[first + b]).astype(F32)
    live[...] = (lane % BLK < bound).astype(F32)

    wide = choose.shape[1]
    r = lax.broadcasted_iota(jnp.int32, (per, 128), 0)
    lane = lax.broadcasted_iota(jnp.int32, (per, 128), 1)
    scene_row = r - asked
    scene_take = (scene_row // (per - asked) * 0) + scene_row // ((per - asked) // SIDE) * piece
    scene_take = scene_take + held + scene_row % ((per - asked) // SIDE)
    for d in range(PLANE):
        seq_index = (d // SIDE * SIDE + z) * SIDE + d % SIDE
        take = scene_take
        for i in range(requests):
            c = request(seq_index, i)
            owner = c // blocks
            far = (owner // SIDE % SIDE + SIDE - z) % SIDE
            slot = jnp.where(far == 3, 1, jnp.where(far == 1, 2, jnp.where(far == 2, 3, 0)))
            inside = owner // PLANE * SIDE + owner % SIDE
            base = slot * piece + inside * (TAKE * blocks) + c % blocks * TAKE
            take = jnp.where(r // TAKE == i, base + r % TAKE, take)
        for w in range(0, wide, 128):
            cols = min(128, wide - w)
            hit = (take == lane + w).astype(F32).astype(BF16)
            choose[d * per : (d + 1) * per, w : w + cols] = hit[:, :cols]


def groups_of(choose, requests):
    return (choose.shape[0] // PLANE - requests * TAKE) // SIDE


def plan(place, counts, pattern, tokens, per, piece):
    smem = pl.BlockSpec(memory_space=pltpu.SMEM)
    rows = tokens + PLANE * per
    return pl.pallas_call(
        plan_kernel,
        in_specs=[smem, smem, smem],
        out_shape=[
            jax.ShapeDtypeStruct((rows, tokens), F32),
            jax.ShapeDtypeStruct((8, tokens), F32),
            jax.ShapeDtypeStruct((tokens, DH), F32),
            jax.ShapeDtypeStruct((PLANE * per, SIDE * piece), BF16),
        ],
        name="plan",
    )(place, counts, pattern)


def choose_kernel(pick, x, out):
    out[...] = nn(pick[...], x[...]).astype(BF16)


def gather_kernel(pick, x, out):
    out[...] = tn(pick[...], x[...])


def attention_kernel(*refs):
    bias, live, live_col, q, go, k, v, got_k, got_v = refs[:9]
    att, dq, d_own, d_got = refs[-4:]
    tokens = q.shape[0]
    half = d_got.shape[1] // 2
    scale = DH ** (-0.5)
    key = jnp.concatenate([k[...], got_k[...]], axis=0)
    val = jnp.concatenate([v[...], got_v[...]], axis=0)
    query = q[...]
    grad = jnp.where(live_col[...] > 0.0, go[...], jnp.zeros((), BF16))
    s = nt(key, query) * (scale * LOG2E) + bias[...]
    e = jnp.exp2(s - jnp.max(s, axis=0, keepdims=True))
    p = e * (1.0 / jnp.sum(e, axis=0, keepdims=True))
    pb = p.astype(BF16)
    dp = nt(val, grad)
    delta = jnp.sum(p * dp, axis=0, keepdims=True)
    ds = (p * (dp - delta) * scale).astype(BF16)
    att[...] = (tn(val, pb) * live[:1]).T.astype(BF16)
    dq[...] = tn(key, ds).T.astype(BF16)
    for which, (left, right) in enumerate(((ds, query), (pb, grad))):
        d = nn(left, right)
        d_own[which] = d[:tokens]
        start = pl.multiple_of(which * half + pl.program_id(0) * DH, DH)
        d_got[:, pl.ds(start, DH)] = d[tokens:].astype(BF16)


def attention(part, bias, live, live_col, q, go, k, v, got, earlier):
    tokens, features = q.shape
    heads = features // DH // PARTS
    base = part * heads
    rows = got.shape[0]

    def whole(shape):
        return pl.BlockSpec(shape, lambda h: (0,) * len(shape))

    def flat(rows, start=base):
        return pl.BlockSpec((rows, DH), lambda h: (0, h + start))

    args = (bias, live, live_col, q, go, k, v, got, got) + tuple(earlier)
    return pl.pallas_call(
        attention_kernel,
        grid=(heads,),
        in_specs=[whole(bias.shape), whole(live.shape), whole(live_col.shape)]
        + [flat(tokens)] * 4
        + [flat(rows, 0), flat(rows, heads)]
        + [pl.BlockSpec(memory_space=pl.ANY)] * len(earlier),
        out_specs=[
            flat(tokens),
            flat(tokens),
            pl.BlockSpec((2, tokens, DH), lambda h: (0, 0, h + base)),
            whole(got.shape),
        ],
        out_shape=[
            jax.ShapeDtypeStruct((tokens, features), BF16),
            jax.ShapeDtypeStruct((tokens, features), BF16),
            jax.ShapeDtypeStruct((2, tokens, features), F32),
            jax.ShapeDtypeStruct(got.shape, BF16),
        ],
        input_output_aliases={9 + i: i for i in range(len(earlier))},
        compiler_params=pltpu.CompilerParams(vmem_limit_bytes=48 << 20),
        name="attention_%d" % part,
    )(*args)


def final_kernel(*refs):
    own, back = refs[:2]
    outs = refs[-2:]
    tokens, width = outs[0].shape
    t = lax.broadcasted_iota(jnp.int32, (tokens, tokens), 0)
    c = lax.broadcasted_iota(jnp.int32, (tokens, tokens), 1)
    order = (holder_row(t, tokens // BLK) == c).astype(F32).astype(BF16)
    for which, out in enumerate(outs):
        far = nn(order, back[:, which * width : (which + 1) * width])
        out[...] = (own[which] + far).astype(BF16)


def final(part, own, back, earlier):
    _, tokens, features = own.shape
    width = features // PARTS
    return pl.pallas_call(
        final_kernel,
        grid=(1,),
        in_specs=[
            pl.BlockSpec((2, tokens, width), lambda i: (0, 0, part)),
            pl.BlockSpec((tokens, 2 * width), lambda i: (0, 0)),
        ]
        + [pl.BlockSpec(memory_space=pl.ANY)] * len(earlier),
        out_specs=[pl.BlockSpec((tokens, width), lambda i: (0, part))] * 2,
        out_shape=[jax.ShapeDtypeStruct((tokens, features), BF16)] * 2,
        input_output_aliases={2 + i: i for i in range(len(earlier))},
        name="final_%d" % part,
    )(own, back, *earlier)


def per_device(queries, keys, values, grad_out, scene_keys, scene_values, valid, pattern):
    groups = lax.axis_size("head")
    position = lax.axis_index("seq")
    tokens, features = queries.shape
    blocks = tokens // BLK
    requests = blocks * RAND + 2
    per = requests * TAKE + SIDE * groups
    width = features // PARTS
    held = PLANE * blocks * TAKE
    piece = held + SCENE_PAD
    cut = (piece // 2 + 7) // 8 * 8

    scene = jnp.concatenate(
        [scene_keys.reshape(groups, features), scene_values.reshape(groups, features)], axis=1
    )
    scene = lax.all_to_all(scene, "head", split_axis=0, concat_axis=0, tiled=True)
    scene = jnp.pad(scene, ((0, SCENE_PAD - groups), (0, 0)))

    bias, live, live_col, pick = plan(
        position.reshape(1), valid, pattern, tokens, per, piece
    )
    got = []
    for part, out in enumerate(spread(keys, values)):
        mine = exchange(out.reshape(PLANE, blocks * TAKE, 2 * width)).reshape(held, 2 * width)
        mine = jnp.concatenate(
            [
                mine,
                jnp.concatenate(
                    [
                        scene[:, part * width : (part + 1) * width],
                        scene[:, features + part * width : features + (part + 1) * width],
                    ],
                    axis=1,
                ),
            ],
            axis=0,
        )
        up = shift_z(mine, 1)
        down = shift_z(mine, -1)
        far_up = shift_z(up[:cut], 1)
        far_down = shift_z(down[cut:], -1)
        pool = jnp.concatenate([mine, up, down, far_up, far_down], axis=0)
        out = jnp.einsum("rc,cf->rf", pick, pool, preferred_element_type=F32).astype(BF16)
        got.append(exchange(out.reshape(PLANE, per, 2 * width)).reshape(PLANE * per, 2 * width))

    results = ()
    back = []
    for part in range(PARTS):
        *results, d_got = attention(
            part, bias, live, live_col, queries, grad_out, keys, values, got[part], results
        )
        back.append(exchange(d_got.reshape(PLANE, per, 2 * width)))
    attended, grad_query, d_own = results

    grads = ()
    scene_back = []
    for part in range(PARTS):
        pool = jnp.einsum(
            "rc,rf->cf",
            pick,
            back[part].reshape(PLANE * per, 2 * width),
            preferred_element_type=F32,
        )
        mine = pool[:piece]
        up = pool[piece : 2 * piece]
        down = pool[2 * piece : 3 * piece]
        far = pool[3 * piece :].astype(BF16)
        far_up = shift_z(far[:cut], -1).astype(F32)
        far_down = shift_z(far[cut:], 1).astype(F32)
        up = jnp.concatenate([up[:cut] + far_up, up[cut:]], axis=0).astype(BF16)
        down = jnp.concatenate([down[:cut], down[cut:] + far_down], axis=0).astype(BF16)
        mine = mine + shift_z(up, -1).astype(F32) + shift_z(down, 1).astype(F32)
        scene_back.append(mine[held : held + groups])
        mine = mine[:held].astype(BF16)
        mine = exchange(mine.reshape(PLANE, blocks * TAKE, 2 * width)).reshape(tokens, 2 * width)
        grads = final(part, d_own, mine, grads)
    scene_back = jnp.concatenate(
        [x[:, :width] for x in scene_back] + [x[:, width:] for x in scene_back], axis=1
    )
    scene_back = lax.all_to_all(
        scene_back.astype(BF16), "head", split_axis=0, concat_axis=0, tiled=True
    )
    grad_scene_keys = scene_back[:, :features].reshape(1, groups * features)
    grad_scene_values = scene_back[:, features:].reshape(1, groups * features)
    return (attended, grad_query, grads[0], grads[1], grad_scene_keys, grad_scene_values)


def solution(mesh):
    block = P("seq", "head")
    rows = P(("seq", "head"), None)
    return jax.shard_map(
        per_device,
        mesh=mesh,
        in_specs=(block, block, block, block, rows, rows, P(), P()),
        out_specs=(block, block, block, block, rows, rows),
        check_vma=False,
    )
```

```python
import jax
import jax.numpy as jnp
from jax import lax
from jax.experimental import pallas as pl
from jax.experimental.pallas import tpu as pltpu
from jax.sharding import PartitionSpec as P


DH = 128
BLK = 64
RAND = 3
SIDE = 4
PLANE = SIDE * SIDE
GROUP = 2 * PLANE
TAKE = BLK // PLANE
F32 = jnp.float32
BF16 = jnp.bfloat16
LOG2E = 1.4426950408889634


def ring_shift(x, stride, by):
    pairs = []
    for i in range(lax.axis_size("seq")):
        c = i // stride % SIDE
        pairs.append((i, i + ((c + by) % SIDE - c) * stride))
    return lax.ppermute(x, "seq", pairs)


def passed_along(x, by):
    length = lax.axis_size("seq")
    pairs = [(i, i + by) for i in range(length) if 0 <= i + by < length]
    return lax.ppermute(x, "seq", pairs)


def head_shift(x, by):
    count = lax.axis_size("head")
    return lax.ppermute(x, "head", [(i, (i + by) % count) for i in range(count)])


def gather_axis(x, stride):
    pieces = [x]
    for s in range(1, SIDE):
        pieces.append(ring_shift(x, stride, s))
    return jnp.concatenate(pieces, axis=0)


def scatter_axis(x, stride):
    rows = x.shape[1] // SIDE
    kind = BF16 if stride == 1 else F32
    total = x[:, :rows]
    for s in range(1, SIDE):
        piece = x[:, s * rows : (s + 1) * rows].astype(kind)
        piece = ring_shift(piece, stride, SIDE - s)
        total = total + piece.astype(F32)
    return total


def exchange(x):
    return lax.all_to_all(x, "seq", split_axis=0, concat_axis=0, tiled=True)


def pair_exchange(x):
    groups = [
        [
            (y * SIDE + z + half) * SIDE + c
            for half in range(2)
            for y in range(SIDE)
            for c in range(SIDE)
        ]
        for z in range(0, SIDE, 2)
    ]
    return lax.all_to_all(
        x, "seq", split_axis=0, concat_axis=0, axis_index_groups=groups, tiled=True
    )


def nt(a, b):
    return lax.dot_general(a, b, (((1,), (1,)), ((), ())), preferred_element_type=F32)


def nn(a, b):
    return lax.dot_general(a, b, (((1,), (0,)), ((), ())), preferred_element_type=F32)


def tn(a, b):
    return lax.dot_general(a, b, (((0,), (0,)), ((), ())), preferred_element_type=F32)


def holder_row(token, blocks):
    return (token % BLK) // TAKE * (TAKE * blocks) + token // BLK * TAKE + token % TAKE


def spread_kernel(k, v, out):
    tokens = k.shape[0]
    r = lax.broadcasted_iota(jnp.int32, (tokens, tokens), 0)
    t = lax.broadcasted_iota(jnp.int32, (tokens, tokens), 1)
    order = (holder_row(t, tokens // BLK) == r).astype(F32).astype(BF16)
    run = tokens // SIDE
    for which, x in enumerate((k, v)):
        moved = nn(order, x[...]).astype(BF16)
        for y in range(SIDE):
            for z in range(which, SIDE, 2):
                start = (y * SIDE + z) * run
                out[start : start + run] = moved[y * run : (y + 1) * run]


def spread(k, v):
    tokens, features = k.shape
    width = 2 * DH
    return pl.pallas_call(
        spread_kernel,
        grid=(features // width,),
        in_specs=[pl.BlockSpec((tokens, width), lambda i: (0, i))] * 2,
        out_specs=pl.BlockSpec((SIDE * tokens, width), lambda i: (0, i)),
        out_shape=jax.ShapeDtypeStruct((SIDE * tokens, features), BF16),
        name="spread",
    )(k, v)


def plan_kernel(place, counts, pattern, bias, live, live_col, choose):
    rows, tokens = bias.shape
    blocks = tokens // BLK
    total = counts.shape[0]
    position = place[0]
    first = position * blocks
    requests = blocks * RAND
    asked = requests * TAKE

    query_block = lax.broadcasted_iota(jnp.int32, (BLK, tokens), 1) // BLK
    offset = lax.broadcasted_iota(jnp.int32, (BLK, tokens), 0)
    for w in range(blocks + 2):
        block = first + (w - 1)
        count = counts[jnp.minimum(jnp.maximum(block, 0), total - 1)]
        count = jnp.where((block >= 0) & (block < total), count, 0)
        ok = (offset < count) & (query_block <= w) & (query_block + 2 >= w)
        bias[w * BLK : (w + 1) * BLK] = jnp.where(ok, 0.0, -1e30).astype(F32)
    near = (blocks + 2) * BLK
    r = lax.broadcasted_iota(jnp.int32, (asked, tokens), 0)
    column_block = lax.broadcasted_iota(jnp.int32, (asked, tokens), 1) // BLK
    count = jnp.zeros((asked, tokens), jnp.int32)
    for i in range(requests):
        here = (r // TAKE == i) & (column_block == i // RAND)
        count = jnp.where(here, counts[pattern[first + i // RAND, i % RAND]], count)
    for g in range(PLANE):
        ok = r % TAKE + g * TAKE < count
        start = near + g * asked
        bias[start : start + asked] = jnp.where(ok, 0.0, -1e30).astype(F32)
    near = near + PLANE * asked
    bias[near:] = jnp.zeros((rows - near, tokens), F32)

    lane = lax.broadcasted_iota(jnp.int32, (8, tokens), 1)
    bound = jnp.zeros((8, tokens), jnp.int32)
    row = lax.broadcasted_iota(jnp.int32, (BLK, DH), 0)
    for b in range(blocks):
        bound = jnp.where(lane // BLK == b, counts[first + b], bound)
        live_col[b * BLK : (b + 1) * BLK] = (row < counts[first + b]).astype(F32)
    live[...] = (lane % BLK < bound).astype(F32)

    z = position // SIDE % SIDE // 2 * 2
    r = lax.broadcasted_iota(jnp.int32, (asked, 128), 0)
    lane = lax.broadcasted_iota(jnp.int32, (asked, 128), 1)
    for d in range(GROUP):
        half, y, x = d // PLANE, d // SIDE % SIDE, d % SIDE
        start = ((y * SIDE + z + half) * SIDE + x) * blocks
        take = r % TAKE
        for i in range(requests):
            base = pattern[start + i // RAND, i % RAND] * TAKE
            take = jnp.where(r // TAKE == i, base + r % TAKE, take)
        for w in range(0, choose.shape[1], 128):
            hit = (take == lane + w).astype(F32).astype(BF16)
            choose[d * asked : (d + 1) * asked, w : w + 128] = hit


def plan(place, counts, pattern, tokens, scene_rows):
    smem = pl.BlockSpec(memory_space=pltpu.SMEM)
    blocks = tokens // BLK
    asked = blocks * RAND * TAKE
    rows = (blocks + 2) * BLK + PLANE * asked + scene_rows
    return pl.pallas_call(
        plan_kernel,
        in_specs=[smem, smem, smem],
        out_shape=[
            jax.ShapeDtypeStruct((rows, tokens), F32),
            jax.ShapeDtypeStruct((8, tokens), F32),
            jax.ShapeDtypeStruct((tokens, DH), F32),
            jax.ShapeDtypeStruct((GROUP * asked, counts.shape[0] * TAKE), BF16),
        ],
        name="plan",
    )(place, counts, pattern)


def attention_kernel(
    bias, live, live_col, q, go, k, v, lo, hi, rnd, scn_k, scn_v, att, dq, d_own, d_halo, d_scn, d_rnd
):
    tokens = q.shape[0]
    far = rnd.shape[1]
    scale = DH ** (-0.5)
    key = jnp.concatenate([lo[0], k[...], hi[0], rnd[0], scn_k[...]], axis=0)
    val = jnp.concatenate([lo[1], v[...], hi[1], rnd[1], scn_v[...]], axis=0)
    query = q[...]
    grad = jnp.where(live_col[...] > 0.0, go[...], jnp.zeros((), BF16))
    s = nt(key, query) * (scale * LOG2E) + bias[...]
    e = jnp.exp2(s - jnp.max(s, axis=0, keepdims=True))
    p = e * (1.0 / jnp.sum(e, axis=0, keepdims=True))
    pb = p.astype(BF16)
    dp = nt(val, grad)
    delta = jnp.sum(p * dp, axis=0, keepdims=True)
    ds = (p * (dp - delta) * scale).astype(BF16)
    att[...] = (tn(val, pb) * live[:1]).T.astype(BF16)
    dq[...] = tn(key, ds).T.astype(BF16)
    for which, (left, right) in enumerate(((ds, query), (pb, grad))):
        d = nn(left, right)
        d_halo[which, :BLK] = d[:BLK].astype(BF16)
        d_own[which] = d[BLK : BLK + tokens]
        d_halo[which, BLK:] = d[BLK + tokens : 2 * BLK + tokens].astype(BF16)
        d_rnd[which] = d[2 * BLK + tokens : 2 * BLK + tokens + far].astype(BF16)
        d_scn[which] = d[2 * BLK + tokens + far :]


def attention(bias, live, live_col, q, go, k, v, lo, hi, rnd, scn):
    tokens, features = q.shape
    heads = features // DH
    far = rnd.shape[1]
    scene = scn.shape[0]

    def whole(x):
        return pl.BlockSpec(x.shape, lambda h: (0,) * x.ndim)

    def flat(rows, start=0):
        return pl.BlockSpec((rows, DH), lambda h: (0, h + start))

    def pair(rows):
        return pl.BlockSpec((2, rows, DH), lambda h: (0, 0, h))

    def shaped(shape, dtype):
        return jax.ShapeDtypeStruct(shape, dtype)

    return pl.pallas_call(
        attention_kernel,
        grid=(heads,),
        in_specs=[whole(bias), whole(live), whole(live_col)]
        + [flat(tokens)] * 4
        + [pair(BLK), pair(BLK), pair(far), flat(scene), flat(scene, heads)],
        out_specs=[
            flat(tokens),
            flat(tokens),
            pair(tokens),
            pair(2 * BLK),
            pair(scene),
            pair(far),
        ],
        out_shape=[
            shaped((tokens, features), BF16),
            shaped((tokens, features), BF16),
            shaped((2, tokens, features), F32),
            shaped((2, 2 * BLK, features), BF16),
            shaped((2, scene, features), F32),
            shaped((2, far, features), BF16),
        ],
        compiler_params=pltpu.CompilerParams(vmem_limit_bytes=48 << 20),
        name="attention",
    )(bias, live, live_col, q, go, k, v, lo, hi, rnd, scn, scn)


def final_kernel(own, back, left, right, *outs):
    tokens = own.shape[1]
    run = tokens // SIDE
    t = lax.broadcasted_iota(jnp.int32, (tokens, tokens), 0)
    c = lax.broadcasted_iota(jnp.int32, (tokens, tokens), 1)
    order = (holder_row(t, tokens // BLK) == c).astype(F32).astype(BF16)
    order = jnp.concatenate([order, order], axis=1)
    for which, out in enumerate(outs):
        starts = [
            (y * SIDE + z) * run for z in range(which, SIDE, 2) for y in range(SIDE)
        ]
        total = own[which] + nn(
            order, jnp.concatenate([back[start : start + run] for start in starts], axis=0)
        )
        edge = jnp.zeros((tokens - BLK, total.shape[1]), F32)
        total = total + jnp.concatenate([left[which].astype(F32), edge], axis=0)
        total = total + jnp.concatenate([edge, right[which].astype(F32)], axis=0)
        out[...] = total.astype(BF16)


def final(own, back, left, right):
    _, tokens, features = own.shape
    width = 2 * DH

    def pair(rows):
        return pl.BlockSpec((2, rows, width), lambda i: (0, 0, i))

    def flat(rows):
        return pl.BlockSpec((rows, width), lambda i: (0, i))

    return pl.pallas_call(
        final_kernel,
        grid=(features // width,),
        in_specs=[pair(tokens), flat(back.shape[0]), pair(BLK), pair(BLK)],
        out_specs=[flat(tokens)] * 2,
        out_shape=[jax.ShapeDtypeStruct((tokens, features), BF16)] * 2,
        name="final",
    )(own, back, left, right)


def program(queries, keys, values, grad_out, scene_keys, scene_values, valid, pattern):
    seq = lax.axis_size("seq")
    groups = lax.axis_size("head")
    group = lax.axis_index("head")
    position = lax.axis_index("seq")
    tokens, features = queries.shape
    blocks = tokens // BLK
    asked = blocks * RAND * TAKE
    axes = (SIDE, SIDE * SIDE, 1)

    out_1 = spread(keys, values)
    in_1 = exchange(out_1.reshape(seq, blocks * TAKE, features))

    both = [x.reshape(groups, features) for x in (scene_keys, scene_values)]
    scn = []
    for s in range(groups):
        to = (group + s) % groups
        row = jnp.concatenate([lax.dynamic_slice_in_dim(x, to, 1, 0) for x in both], axis=1)
        scn.append(head_shift(row, s) if s else row)
    scn = jnp.concatenate(scn, axis=0)
    for stride in axes:
        scn = gather_axis(scn, stride)
    lo = jnp.stack([keys[tokens - BLK :], values[tokens - BLK :]])
    hi = jnp.stack([keys[:BLK], values[:BLK]])
    lo = passed_along(lo, 1)
    hi = passed_along(hi, -1)

    bias, live, live_col, pick = plan(
        position.reshape(1), valid, pattern, tokens, scn.shape[0]
    )
    out_2 = jnp.einsum(
        "rc,cf->rf", pick, in_1.reshape(-1, features), preferred_element_type=F32
    ).astype(BF16)
    rnd = pair_exchange(out_2.reshape(GROUP, asked, features)).reshape(2, -1, features)

    attended, grad_query, d_own, d_halo, d_scn, d_rnd = attention(
        bias, live, live_col, queries, grad_out, keys, values, lo, hi, rnd, scn
    )

    back_1 = pair_exchange(d_rnd.reshape(GROUP, asked, features))
    from_right = passed_along(d_halo[:, :BLK], -1)
    from_left = passed_along(d_halo[:, BLK:], 1)
    for stride in reversed(axes):
        d_scn = scatter_axis(d_scn, stride)
    d_scn = jnp.concatenate([d_scn[0], d_scn[1]], axis=1).astype(BF16)
    totals = [jnp.zeros((groups, features), BF16)] * 2
    for s in range(groups):
        row = d_scn[s : s + 1]
        row = head_shift(row, groups - s) if s else row
        at = (group + s) % groups
        for which in range(2):
            totals[which] = lax.dynamic_update_slice_in_dim(
                totals[which], row[:, which * features : (which + 1) * features], at, 0
            )
    totals = [x.reshape(1, groups * features) for x in totals]

    held = jnp.einsum(
        "rc,rf->cf", pick, back_1.reshape(-1, features), preferred_element_type=F32
    ).astype(BF16)
    back_2 = exchange(held.reshape(seq, blocks * TAKE, features))
    grads = final(d_own, back_2.reshape(-1, features), from_left, from_right)
    return (attended, grad_query, grads[0], grads[1], totals[0], totals[1])


def solution(mesh):
    block = P("seq", "head")
    rows = P(("seq", "head"), None)
    return jax.shard_map(
        program,
        mesh=mesh,
        in_specs=(block, block, block, block, rows, rows, P(), P()),
        out_specs=(block, block, block, block, rows, rows),
        check_vma=False,
    )
```

```python
import jax
import jax.numpy as jnp
from jax import lax
from jax.experimental import pallas as pl
from jax.experimental.pallas import tpu as pltpu
from jax.sharding import PartitionSpec as P


DH = 128
BLK = 64
RAND = 3
SIDE = 4
HOLD = 32
TAKE = BLK // HOLD
F32 = jnp.float32
BF16 = jnp.bfloat16
LOG2E = 1.4426950408889634


def ring_shift(x, stride, by):
    pairs = []
    for i in range(lax.axis_size("seq")):
        c = i // stride % SIDE
        pairs.append((i, i + ((c + by) % SIDE - c) * stride))
    return lax.ppermute(x, "seq", pairs)


def passed_along(x, by):
    length = lax.axis_size("seq")
    pairs = [(i, i + by) for i in range(length) if 0 <= i + by < length]
    return lax.ppermute(x, "seq", pairs)


def head_shift(x, by):
    count = lax.axis_size("head")
    return lax.ppermute(x, "head", [(i, (i + by) % count) for i in range(count)])


def gather_axis(x, stride):
    pieces = [x]
    for s in range(1, SIDE):
        pieces.append(ring_shift(x, stride, s))
    return jnp.concatenate(pieces, axis=0)


def scatter_axis(x, stride):
    rows = x.shape[1] // SIDE
    kind = BF16 if stride == 1 else F32
    total = x[:, :rows]
    for s in range(1, SIDE):
        piece = x[:, s * rows : (s + 1) * rows].astype(kind)
        piece = ring_shift(piece, stride, SIDE - s)
        total = total + piece.astype(F32)
    return total


def exchange(x):
    return lax.all_to_all(x, "seq", split_axis=0, concat_axis=0, tiled=True)


def nt(a, b):
    return lax.dot_general(a, b, (((1,), (1,)), ((), ())), preferred_element_type=F32)


def nn(a, b):
    return lax.dot_general(a, b, (((1,), (0,)), ((), ())), preferred_element_type=F32)


def tn(a, b):
    return lax.dot_general(a, b, (((0,), (0,)), ((), ())), preferred_element_type=F32)


def holder_row(token, blocks):
    return (token % BLK) // TAKE * (TAKE * blocks) + token // BLK * TAKE + token % TAKE


def spread_kernel(k, v, out):
    tokens = k.shape[0]
    r = lax.broadcasted_iota(jnp.int32, (tokens, tokens), 0)
    t = lax.broadcasted_iota(jnp.int32, (tokens, tokens), 1)
    order = (holder_row(t, tokens // BLK) == r).astype(F32).astype(BF16)
    out[:tokens] = nn(order, k[...]).astype(BF16)
    out[tokens:] = nn(order, v[...]).astype(BF16)


def spread(k, v):
    tokens, features = k.shape
    width = 2 * DH
    return pl.pallas_call(
        spread_kernel,
        grid=(features // width,),
        in_specs=[pl.BlockSpec((tokens, width), lambda i: (0, i))] * 2,
        out_specs=pl.BlockSpec((2 * tokens, width), lambda i: (0, i)),
        out_shape=jax.ShapeDtypeStruct((2 * tokens, features), BF16),
        name="spread",
    )(k, v)


def plan_kernel(place, counts, pattern, bias, live, live_col, choose):
    rows, tokens = bias.shape
    blocks = tokens // BLK
    total = counts.shape[0]
    position = place[0]
    first = position * blocks
    requests = blocks * RAND
    asked = requests * TAKE

    query_block = lax.broadcasted_iota(jnp.int32, (BLK, tokens), 1) // BLK
    offset = lax.broadcasted_iota(jnp.int32, (BLK, tokens), 0)
    for w in range(blocks + 2):
        block = first + (w - 1)
        count = counts[jnp.minimum(jnp.maximum(block, 0), total - 1)]
        count = jnp.where((block >= 0) & (block < total), count, 0)
        ok = (offset < count) & (query_block <= w) & (query_block + 2 >= w)
        bias[w * BLK : (w + 1) * BLK] = jnp.where(ok, 0.0, -1e30).astype(F32)
    near = (blocks + 2) * BLK
    r = lax.broadcasted_iota(jnp.int32, (asked, tokens), 0)
    column_block = lax.broadcasted_iota(jnp.int32, (asked, tokens), 1) // BLK
    count = jnp.zeros((asked, tokens), jnp.int32)
    for i in range(requests):
        here = (r // TAKE == i) & (column_block == i // RAND)
        count = jnp.where(here, counts[pattern[first + i // RAND, i % RAND]], count)
    for g in range(HOLD):
        ok = r % TAKE + g * TAKE < count
        start = near + g * asked
        bias[start : start + asked] = jnp.where(ok, 0.0, -1e30).astype(F32)
    near = near + HOLD * asked
    bias[near:] = jnp.zeros((rows - near, tokens), F32)

    lane = lax.broadcasted_iota(jnp.int32, (8, tokens), 1)
    bound = jnp.zeros((8, tokens), jnp.int32)
    row = lax.broadcasted_iota(jnp.int32, (BLK, DH), 0)
    for b in range(blocks):
        bound = jnp.where(lane // BLK == b, counts[first + b], bound)
        live_col[b * BLK : (b + 1) * BLK] = (row < counts[first + b]).astype(F32)
    live[...] = (lane % BLK < bound).astype(F32)

    r = lax.broadcasted_iota(jnp.int32, (asked, 128), 0)
    lane = lax.broadcasted_iota(jnp.int32, (asked, 128), 1)
    for d in range(total // blocks):
        start = d * blocks
        take = r % TAKE
        for i in range(requests):
            base = pattern[start + i // RAND, i % RAND] * TAKE
            take = jnp.where(r // TAKE == i, base + r % TAKE, take)
        for w in range(0, choose.shape[1], 128):
            hit = (take == lane + w).astype(F32).astype(BF16)
            choose[d * asked : (d + 1) * asked, w : w + 128] = hit


def plan(place, counts, pattern, tokens, scene_rows):
    smem = pl.BlockSpec(memory_space=pltpu.SMEM)
    blocks = tokens // BLK
    asked = blocks * RAND * TAKE
    rows = (blocks + 2) * BLK + HOLD * asked + scene_rows
    return pl.pallas_call(
        plan_kernel,
        in_specs=[smem, smem, smem],
        out_shape=[
            jax.ShapeDtypeStruct((rows, tokens), F32),
            jax.ShapeDtypeStruct((8, tokens), F32),
            jax.ShapeDtypeStruct((tokens, DH), F32),
            jax.ShapeDtypeStruct((2 * HOLD * asked, counts.shape[0] * TAKE), BF16),
        ],
        name="plan",
    )(place, counts, pattern)


def attention_kernel(
    bias, live, live_col, q, go, k, v, lo, hi, rnd, scn_k, scn_v, att, dq, d_own, d_halo, d_scn, d_rnd
):
    tokens = q.shape[0]
    far = rnd.shape[1]
    scale = DH ** (-0.5)
    key = jnp.concatenate([lo[0], k[...], hi[0], rnd[0], scn_k[...]], axis=0)
    val = jnp.concatenate([lo[1], v[...], hi[1], rnd[1], scn_v[...]], axis=0)
    query = q[...]
    grad = jnp.where(live_col[...] > 0.0, go[...], jnp.zeros((), BF16))
    s = nt(key, query) * (scale * LOG2E) + bias[...]
    e = jnp.exp2(s - jnp.max(s, axis=0, keepdims=True))
    p = e * (1.0 / jnp.sum(e, axis=0, keepdims=True))
    pb = p.astype(BF16)
    dp = nt(val, grad)
    delta = jnp.sum(p * dp, axis=0, keepdims=True)
    ds = (p * (dp - delta) * scale).astype(BF16)
    att[...] = (tn(val, pb) * live[:1]).T.astype(BF16)
    dq[...] = tn(key, ds).T.astype(BF16)
    for which, (left, right) in enumerate(((ds, query), (pb, grad))):
        d = nn(left, right)
        d_halo[which, :BLK] = d[:BLK].astype(BF16)
        d_own[which] = d[BLK : BLK + tokens]
        d_halo[which, BLK:] = d[BLK + tokens : 2 * BLK + tokens].astype(BF16)
        d_rnd[which] = d[2 * BLK + tokens : 2 * BLK + tokens + far].astype(BF16)
        d_scn[which] = d[2 * BLK + tokens + far :]


def attention(bias, live, live_col, q, go, k, v, lo, hi, rnd, scn):
    tokens, features = q.shape
    heads = features // DH
    far = rnd.shape[1]
    scene = scn.shape[0]

    def whole(x):
        return pl.BlockSpec(x.shape, lambda h: (0,) * x.ndim)

    def flat(rows, start=0):
        return pl.BlockSpec((rows, DH), lambda h: (0, h + start))

    def pair(rows):
        return pl.BlockSpec((2, rows, DH), lambda h: (0, 0, h))

    def shaped(shape, dtype):
        return jax.ShapeDtypeStruct(shape, dtype)

    return pl.pallas_call(
        attention_kernel,
        grid=(heads,),
        in_specs=[whole(bias), whole(live), whole(live_col)]
        + [flat(tokens)] * 4
        + [pair(BLK), pair(BLK), pair(far), flat(scene), flat(scene, heads)],
        out_specs=[
            flat(tokens),
            flat(tokens),
            pair(tokens),
            pair(2 * BLK),
            pair(scene),
            pair(far),
        ],
        out_shape=[
            shaped((tokens, features), BF16),
            shaped((tokens, features), BF16),
            shaped((2, tokens, features), F32),
            shaped((2, 2 * BLK, features), BF16),
            shaped((2, scene, features), F32),
            shaped((2, far, features), BF16),
        ],
        compiler_params=pltpu.CompilerParams(vmem_limit_bytes=48 << 20),
        name="attention",
    )(bias, live, live_col, q, go, k, v, lo, hi, rnd, scn, scn)


def final_kernel(own, back, left, right, *outs):
    tokens = own.shape[1]
    t = lax.broadcasted_iota(jnp.int32, (tokens, tokens), 0)
    c = lax.broadcasted_iota(jnp.int32, (tokens, tokens), 1)
    order = (holder_row(t, tokens // BLK) == c).astype(F32).astype(BF16)
    for which, out in enumerate(outs):
        total = own[which] + nn(order, back[which * tokens : (which + 1) * tokens])
        edge = jnp.zeros((tokens - BLK, total.shape[1]), F32)
        total = total + jnp.concatenate([left[which].astype(F32), edge], axis=0)
        total = total + jnp.concatenate([edge, right[which].astype(F32)], axis=0)
        out[...] = total.astype(BF16)


def final(own, back, left, right):
    _, tokens, features = own.shape
    width = 2 * DH

    def pair(rows):
        return pl.BlockSpec((2, rows, width), lambda i: (0, 0, i))

    def flat(rows):
        return pl.BlockSpec((rows, width), lambda i: (0, i))

    return pl.pallas_call(
        final_kernel,
        grid=(features // width,),
        in_specs=[pair(tokens), flat(back.shape[0]), pair(BLK), pair(BLK)],
        out_specs=[flat(tokens)] * 2,
        out_shape=[jax.ShapeDtypeStruct((tokens, features), BF16)] * 2,
        name="final",
    )(own, back, left, right)


def program(queries, keys, values, grad_out, scene_keys, scene_values, valid, pattern):
    seq = lax.axis_size("seq")
    groups = lax.axis_size("head")
    group = lax.axis_index("head")
    position = lax.axis_index("seq")
    tokens, features = queries.shape
    blocks = tokens // BLK
    asked = blocks * RAND * TAKE
    axes = (SIDE, SIDE * SIDE, 1)

    out_1 = spread(keys, values)
    in_1 = exchange(out_1.reshape(seq, blocks * TAKE, features))

    both = [x.reshape(groups, features) for x in (scene_keys, scene_values)]
    scn = []
    for s in range(groups):
        to = (group + s) % groups
        row = jnp.concatenate([lax.dynamic_slice_in_dim(x, to, 1, 0) for x in both], axis=1)
        scn.append(head_shift(row, s) if s else row)
    scn = jnp.concatenate(scn, axis=0)
    for stride in axes:
        scn = gather_axis(scn, stride)
    lo = jnp.stack([keys[tokens - BLK :], values[tokens - BLK :]])
    hi = jnp.stack([keys[:BLK], values[:BLK]])
    lo = passed_along(lo, 1)
    hi = passed_along(hi, -1)

    bias, live, live_col, pick = plan(
        position.reshape(1), valid, pattern, tokens, scn.shape[0]
    )
    out_2 = jnp.einsum(
        "rc,cf->rf", pick, in_1.reshape(-1, features), preferred_element_type=F32
    ).astype(BF16)
    rnd = exchange(out_2.reshape(seq, asked, features)).reshape(2, -1, features)

    attended, grad_query, d_own, d_halo, d_scn, d_rnd = attention(
        bias, live, live_col, queries, grad_out, keys, values, lo, hi, rnd, scn
    )

    back_1 = exchange(d_rnd.reshape(seq, asked, features))
    from_right = passed_along(d_halo[:, :BLK], -1)
    from_left = passed_along(d_halo[:, BLK:], 1)
    for stride in reversed(axes):
        d_scn = scatter_axis(d_scn, stride)
    d_scn = jnp.concatenate([d_scn[0], d_scn[1]], axis=1).astype(BF16)
    totals = [jnp.zeros((groups, features), BF16)] * 2
    for s in range(groups):
        row = d_scn[s : s + 1]
        row = head_shift(row, groups - s) if s else row
        at = (group + s) % groups
        for which in range(2):
            totals[which] = lax.dynamic_update_slice_in_dim(
                totals[which], row[:, which * features : (which + 1) * features], at, 0
            )
    totals = [x.reshape(1, groups * features) for x in totals]

    held = jnp.einsum(
        "rc,rf->cf", pick, back_1.reshape(-1, features), preferred_element_type=F32
    ).astype(BF16)
    back_2 = exchange(held.reshape(seq, blocks * TAKE, features))
    grads = final(d_own, back_2.reshape(-1, features), from_left, from_right)
    return (attended, grad_query, grads[0], grads[1], totals[0], totals[1])


def solution(mesh):
    block = P("seq", "head")
    rows = P(("seq", "head"), None)
    return jax.shard_map(
        program,
        mesh=mesh,
        in_specs=(block, block, block, block, rows, rows, P(), P()),
        out_specs=(block, block, block, block, rows, rows),
        check_vma=False,
    )
```

```python
import jax
import jax.numpy as jnp
from jax import lax
from jax.experimental import pallas as pl
from jax.experimental.pallas import tpu as pltpu
from jax.sharding import PartitionSpec as P


DH = 128
BLK = 64
RAND = 3
SIDE = 4
HOLD = 32
TAKE = BLK // HOLD
F32 = jnp.float32
BF16 = jnp.bfloat16
LOG2E = 1.4426950408889634


def ring_shift(x, stride, by):
    pairs = []
    for i in range(lax.axis_size("seq")):
        c = i // stride % SIDE
        pairs.append((i, i + ((c + by) % SIDE - c) * stride))
    return lax.ppermute(x, "seq", pairs)


def passed_along(x, by):
    length = lax.axis_size("seq")
    pairs = [(i, i + by) for i in range(length) if 0 <= i + by < length]
    return lax.ppermute(x, "seq", pairs)


def scene_exchange(x):
    heads = lax.axis_size("head")
    groups = [
        [
            ((y * SIDE + z) * SIDE + c) * heads + h
            for z in range(SIDE)
            for h in range(heads)
        ]
        for y in range(SIDE)
        for c in range(SIDE)
    ]
    return lax.all_to_all(
        x, ("seq", "head"), split_axis=0, concat_axis=0, axis_index_groups=groups, tiled=True
    )


def gather_axis(x, stride):
    pieces = [x]
    for s in range(1, SIDE):
        pieces.append(ring_shift(x, stride, s))
    return pieces


def scatter_axis(x, stride):
    rows = x.shape[1] // SIDE
    kind = BF16 if stride == 1 else F32
    total = x[:, :rows]
    for s in range(1, SIDE):
        piece = x[:, s * rows : (s + 1) * rows].astype(kind)
        piece = ring_shift(piece, stride, SIDE - s)
        total = total + piece.astype(F32)
    return total


def exchange(x):
    return lax.all_to_all(x, "seq", split_axis=0, concat_axis=0, tiled=True)


def nt(a, b):
    return lax.dot_general(a, b, (((1,), (1,)), ((), ())), preferred_element_type=F32)


def nn(a, b):
    return lax.dot_general(a, b, (((1,), (0,)), ((), ())), preferred_element_type=F32)


def tn(a, b):
    return lax.dot_general(a, b, (((0,), (0,)), ((), ())), preferred_element_type=F32)


def holder_row(token, blocks):
    return (token % BLK) // TAKE * (TAKE * blocks) + token // BLK * TAKE + token % TAKE


def spread_kernel(k, v, out):
    tokens = k.shape[0]
    r = lax.broadcasted_iota(jnp.int32, (tokens, tokens), 0)
    t = lax.broadcasted_iota(jnp.int32, (tokens, tokens), 1)
    order = (holder_row(t, tokens // BLK) == r).astype(F32).astype(BF16)
    out[:tokens] = nn(order, k[...]).astype(BF16)
    out[tokens:] = nn(order, v[...]).astype(BF16)


def spread(k, v):
    tokens, features = k.shape
    width = 2 * DH
    return pl.pallas_call(
        spread_kernel,
        grid=(features // width,),
        in_specs=[pl.BlockSpec((tokens, width), lambda i: (0, i))] * 2,
        out_specs=pl.BlockSpec((2 * tokens, width), lambda i: (0, i)),
        out_shape=jax.ShapeDtypeStruct((2 * tokens, features), BF16),
        name="spread",
    )(k, v)


def plan_kernel(place, counts, pattern, bias, live, live_col, choose):
    rows, tokens = bias.shape
    blocks = tokens // BLK
    total = counts.shape[0]
    position = place[0]
    first = position * blocks
    requests = blocks * RAND
    asked = requests * TAKE

    query_block = lax.broadcasted_iota(jnp.int32, (BLK, tokens), 1) // BLK
    offset = lax.broadcasted_iota(jnp.int32, (BLK, tokens), 0)
    for w in range(blocks + 2):
        block = first + (w - 1)
        count = counts[jnp.minimum(jnp.maximum(block, 0), total - 1)]
        count = jnp.where((block >= 0) & (block < total), count, 0)
        ok = (offset < count) & (query_block <= w) & (query_block + 2 >= w)
        bias[w * BLK : (w + 1) * BLK] = jnp.where(ok, 0.0, -1e30).astype(F32)
    near = (blocks + 2) * BLK
    r = lax.broadcasted_iota(jnp.int32, (asked, tokens), 0)
    column_block = lax.broadcasted_iota(jnp.int32, (asked, tokens), 1) // BLK
    count = jnp.zeros((asked, tokens), jnp.int32)
    for i in range(requests):
        here = (r // TAKE == i) & (column_block == i // RAND)
        count = jnp.where(here, counts[pattern[first + i // RAND, i % RAND]], count)
    for g in range(HOLD):
        ok = r % TAKE + g * TAKE < count
        start = near + g * asked
        bias[start : start + asked] = jnp.where(ok, 0.0, -1e30).astype(F32)
    near = near + HOLD * asked
    bias[near:] = jnp.zeros((rows - near, tokens), F32)

    lane = lax.broadcasted_iota(jnp.int32, (8, tokens), 1)
    bound = jnp.zeros((8, tokens), jnp.int32)
    row = lax.broadcasted_iota(jnp.int32, (BLK, DH), 0)
    for b in range(blocks):
        bound = jnp.where(lane // BLK == b, counts[first + b], bound)
        live_col[b * BLK : (b + 1) * BLK] = (row < counts[first + b]).astype(F32)
    live[...] = (lane % BLK < bound).astype(F32)

    r = lax.broadcasted_iota(jnp.int32, (asked, 128), 0)
    lane = lax.broadcasted_iota(jnp.int32, (asked, 128), 1)
    for d in range(total // blocks):
        start = d * blocks
        take = r % TAKE
        for i in range(requests):
            base = pattern[start + i // RAND, i % RAND] * TAKE
            take = jnp.where(r // TAKE == i, base + r % TAKE, take)
        for w in range(0, choose.shape[1], 128):
            hit = (take == lane + w).astype(F32).astype(BF16)
            choose[d * asked : (d + 1) * asked, w : w + 128] = hit


def plan(place, counts, pattern, tokens, scene_rows):
    smem = pl.BlockSpec(memory_space=pltpu.SMEM)
    blocks = tokens // BLK
    asked = blocks * RAND * TAKE
    rows = (blocks + 2) * BLK + HOLD * asked + scene_rows
    return pl.pallas_call(
        plan_kernel,
        in_specs=[smem, smem, smem],
        out_shape=[
            jax.ShapeDtypeStruct((rows, tokens), F32),
            jax.ShapeDtypeStruct((8, tokens), F32),
            jax.ShapeDtypeStruct((tokens, DH), F32),
            jax.ShapeDtypeStruct((2 * HOLD * asked, counts.shape[0] * TAKE), BF16),
        ],
        name="plan",
    )(place, counts, pattern)


def scores(key, query, bias):
    return nt(key, query) * (DH ** (-0.5) * LOG2E) + bias


def masked_grad(live_col, go):
    return jnp.where(live_col[...] > 0.0, go[...], jnp.zeros((), BF16))


def near_kernel(bias, live_col, q, go, k, v, lo, hi, stats):
    key = jnp.concatenate([lo[0], k[...], hi[0]], axis=0)
    val = jnp.concatenate([lo[1], v[...], hi[1]], axis=0)
    s = scores(key, q[...], bias[: key.shape[0]])
    m = jnp.max(s, axis=0, keepdims=True)
    e = jnp.exp2(s - m)
    stats[0, 0:1] = m
    stats[0, 1:2] = jnp.sum(e, axis=0, keepdims=True)
    dp = nt(val, masked_grad(live_col, go))
    stats[0, 2:3] = jnp.sum(e * dp, axis=0, keepdims=True)


def far_kernel(bias, live_col, q, go, near, rnd, *refs):
    scn_k, scn_v, (d_rnd, d_scn, stats) = refs[:SIDE], refs[SIDE : 2 * SIDE], refs[2 * SIDE :]
    scale = DH ** (-0.5)
    far = rnd.shape[1]
    key = jnp.concatenate([rnd[0]] + [x[...] for x in scn_k], axis=0)
    val = jnp.concatenate([rnd[1]] + [x[...] for x in scn_v], axis=0)
    query = q[...]
    grad = masked_grad(live_col, go)
    s = scores(key, query, bias[bias.shape[0] - key.shape[0] :])
    m = jnp.maximum(near[0, 0:1], jnp.max(s, axis=0, keepdims=True))
    e = jnp.exp2(s - m)
    shrink = jnp.exp2(near[0, 0:1] - m)
    inverse = 1.0 / (near[0, 1:2] * shrink + jnp.sum(e, axis=0, keepdims=True))
    dp = nt(val, grad)
    delta = (near[0, 2:3] * shrink + jnp.sum(e * dp, axis=0, keepdims=True)) * inverse
    stats[0, 0:1] = m
    stats[0, 1:2] = inverse
    stats[0, 2:3] = delta
    p = e * inverse
    d = nn(p.astype(BF16), grad)
    d_rnd[1] = d[:far].astype(BF16)
    d_scn[1] = d[far:]
    d = nn((p * (dp - delta) * scale).astype(BF16), query)
    d_rnd[0] = d[:far].astype(BF16)
    d_scn[0] = d[far:]


def rest_kernel(bias, live, live_col, q, go, stats, k, v, lo, hi, rnd, *refs):
    scn_k, scn_v = refs[:SIDE], refs[SIDE : 2 * SIDE]
    att, dq, d_own, d_halo = refs[2 * SIDE :]
    tokens = q.shape[0]
    window = tokens + 2 * BLK
    scale = DH ** (-0.5)
    key = jnp.concatenate([lo[0], k[...], hi[0], rnd[0]] + [x[...] for x in scn_k], axis=0)
    val = jnp.concatenate([lo[1], v[...], hi[1], rnd[1]] + [x[...] for x in scn_v], axis=0)
    query = q[...]
    grad = masked_grad(live_col, go)
    p = jnp.exp2(scores(key, query, bias[...]) - stats[0, 0:1]) * stats[0, 1:2]
    pb = p.astype(BF16)
    ds = (p * (nt(val, grad) - stats[0, 2:3]) * scale).astype(BF16)
    att[...] = (tn(val, pb) * live[:1]).T.astype(BF16)
    dq[...] = tn(key, ds).T.astype(BF16)
    for which, (left, right) in enumerate(((ds, query), (pb, grad))):
        d = nn(left[:window], right)
        d_halo[which, :BLK] = d[:BLK].astype(BF16)
        d_own[which] = d[BLK : BLK + tokens]
        d_halo[which, BLK:] = d[BLK + tokens :].astype(BF16)


def whole(x):
    return pl.BlockSpec(x.shape, lambda h: (0,) * x.ndim)


def flat(rows, start=0):
    return pl.BlockSpec((rows, DH), lambda h: (0, h + start))


def pair(rows):
    return pl.BlockSpec((2, rows, DH), lambda h: (0, 0, h))


def per_head(tokens):
    return pl.BlockSpec((1, 8, tokens), lambda h: (h, 0, 0))


def shaped(shape, dtype):
    return jax.ShapeDtypeStruct(shape, dtype)


def kernel_call(kernel, heads, args, in_specs, out_specs, out_shape):
    return pl.pallas_call(
        kernel,
        grid=(heads,),
        in_specs=in_specs,
        out_specs=out_specs,
        out_shape=out_shape,
        compiler_params=pltpu.CompilerParams(vmem_limit_bytes=48 << 20),
    )(*args)


def near_part(bias, live_col, q, go, k, v, lo, hi):
    tokens, features = q.shape
    heads = features // DH
    return kernel_call(
        near_kernel,
        heads,
        (bias, live_col, q, go, k, v, lo, hi),
        [whole(bias), whole(live_col)] + [flat(tokens)] * 4 + [pair(BLK)] * 2,
        per_head(tokens),
        shaped((heads, 8, tokens), F32),
    )


def far_part(bias, live_col, q, go, near, rnd, scn):
    tokens, features = q.shape
    heads = features // DH
    far = rnd.shape[1]
    rows = scn[0].shape[0]
    return kernel_call(
        far_kernel,
        heads,
        (bias, live_col, q, go, near, rnd, *scn, *scn),
        [whole(bias), whole(live_col)]
        + [flat(tokens)] * 2
        + [per_head(tokens), pair(far)]
        + [flat(rows)] * SIDE
        + [flat(rows, heads)] * SIDE,
        [pair(far), pair(SIDE * rows), per_head(tokens)],
        [
            shaped((2, far, features), BF16),
            shaped((2, SIDE * rows, features), F32),
            shaped((heads, 8, tokens), F32),
        ],
    )


def rest_part(bias, live, live_col, q, go, stats, k, v, lo, hi, rnd, scn):
    tokens, features = q.shape
    heads = features // DH
    rows = scn[0].shape[0]
    return kernel_call(
        rest_kernel,
        heads,
        (bias, live, live_col, q, go, stats, k, v, lo, hi, rnd, *scn, *scn),
        [whole(bias), whole(live), whole(live_col)]
        + [flat(tokens)] * 2
        + [per_head(tokens)]
        + [flat(tokens)] * 2
        + [pair(BLK), pair(BLK), pair(rnd.shape[1])]
        + [flat(rows)] * SIDE
        + [flat(rows, heads)] * SIDE,
        [flat(tokens), flat(tokens), pair(tokens), pair(2 * BLK)],
        [
            shaped((tokens, features), BF16),
            shaped((tokens, features), BF16),
            shaped((2, tokens, features), F32),
            shaped((2, 2 * BLK, features), BF16),
        ],
    )


def final_kernel(own, back, left, right, *outs):
    tokens = own.shape[1]
    t = lax.broadcasted_iota(jnp.int32, (tokens, tokens), 0)
    c = lax.broadcasted_iota(jnp.int32, (tokens, tokens), 1)
    order = (holder_row(t, tokens // BLK) == c).astype(F32).astype(BF16)
    for which, out in enumerate(outs):
        total = own[which] + nn(order, back[which * tokens : (which + 1) * tokens])
        edge = jnp.zeros((tokens - BLK, total.shape[1]), F32)
        total = total + jnp.concatenate([left[which].astype(F32), edge], axis=0)
        total = total + jnp.concatenate([edge, right[which].astype(F32)], axis=0)
        out[...] = total.astype(BF16)


def final(own, back, left, right):
    _, tokens, features = own.shape
    width = 2 * DH

    def two(rows):
        return pl.BlockSpec((2, rows, width), lambda i: (0, 0, i))

    def one(rows):
        return pl.BlockSpec((rows, width), lambda i: (0, i))

    return pl.pallas_call(
        final_kernel,
        grid=(features // width,),
        in_specs=[two(tokens), one(back.shape[0]), two(BLK), two(BLK)],
        out_specs=[one(tokens)] * 2,
        out_shape=[jax.ShapeDtypeStruct((tokens, features), BF16)] * 2,
        name="final",
    )(own, back, left, right)


def program(queries, keys, values, grad_out, scene_keys, scene_values, valid, pattern):
    seq = lax.axis_size("seq")
    groups = lax.axis_size("head")
    position = lax.axis_index("seq")
    tokens, features = queries.shape
    blocks = tokens // BLK
    asked = blocks * RAND * TAKE
    axes = (SIDE * SIDE, 1)

    scn = jnp.concatenate(
        [x.reshape(groups, features) for x in (scene_keys, scene_values)], axis=1
    )
    scn = scene_exchange(jnp.concatenate([scn] * SIDE, axis=0))

    out_1 = spread(keys, values)
    in_1 = exchange(out_1.reshape(seq, blocks * TAKE, features))

    for stride in axes:
        pieces = gather_axis(scn, stride)
        scn = jnp.concatenate(pieces, axis=0) if stride != axes[-1] else pieces
    lo = jnp.stack([keys[tokens - BLK :], values[tokens - BLK :]])
    hi = jnp.stack([keys[:BLK], values[:BLK]])
    lo = passed_along(lo, 1)
    hi = passed_along(hi, -1)

    bias, live, live_col, pick = plan(
        position.reshape(1), valid, pattern, tokens, seq * groups
    )
    out_2 = jnp.einsum(
        "rc,cf->rf", pick, in_1.reshape(-1, features), preferred_element_type=F32
    ).astype(BF16)
    rnd = exchange(out_2.reshape(seq, asked, features)).reshape(2, -1, features)

    near = near_part(bias, live_col, queries, grad_out, keys, values, lo, hi)
    d_rnd, d_scn, stats = far_part(bias, live_col, queries, grad_out, near, rnd, scn)

    back_1 = exchange(d_rnd.reshape(seq, asked, features))
    attended, grad_query, d_own, d_halo = rest_part(
        bias, live, live_col, queries, grad_out, stats, keys, values, lo, hi, rnd, scn
    )
    from_right = passed_along(d_halo[:, :BLK], -1)
    from_left = passed_along(d_halo[:, BLK:], 1)
    for stride in reversed(axes):
        d_scn = scatter_axis(d_scn, stride)
    d_scn = jnp.concatenate([d_scn[0], d_scn[1]], axis=1).astype(BF16)
    d_scn = scene_exchange(d_scn)
    d_scn = jnp.sum(d_scn.reshape(SIDE, groups, 2 * features).astype(F32), axis=0).astype(BF16)
    totals = [
        d_scn[:, which * features : (which + 1) * features].reshape(1, groups * features)
        for which in range(2)
    ]

    held = jnp.einsum(
        "rc,rf->cf", pick, back_1.reshape(-1, features), preferred_element_type=F32
    ).astype(BF16)
    back_2 = exchange(held.reshape(seq, blocks * TAKE, features))
    grads = final(d_own, back_2.reshape(-1, features), from_left, from_right)
    return (attended, grad_query, grads[0], grads[1], totals[0], totals[1])


def solution(mesh):
    block = P("seq", "head")
    rows = P(("seq", "head"), None)
    return jax.shard_map(
        program,
        mesh=mesh,
        in_specs=(block, block, block, block, rows, rows, P(), P()),
        out_specs=(block, block, block, block, rows, rows),
        check_vma=False,
    )
```

```python
import jax
import jax.numpy as jnp
from jax import lax
from jax.experimental import pallas as pl
from jax.experimental.pallas import tpu as pltpu
from jax.sharding import PartitionSpec as P


DH = 128
BLK = 64
RAND = 3
SIDE = 4
HOLD = 32
TAKE = BLK // HOLD
F32 = jnp.float32
BF16 = jnp.bfloat16
LOG2E = 1.4426950408889634


def ring_shift(x, stride, by):
    pairs = []
    for i in range(lax.axis_size("seq")):
        c = i // stride % SIDE
        pairs.append((i, i + ((c + by) % SIDE - c) * stride))
    return lax.ppermute(x, "seq", pairs)


def passed_along(x, by):
    length = lax.axis_size("seq")
    pairs = [(i, i + by) for i in range(length) if 0 <= i + by < length]
    return lax.ppermute(x, "seq", pairs)


def head_shift(x, by):
    count = lax.axis_size("head")
    return lax.ppermute(x, "head", [(i, (i + by) % count) for i in range(count)])


def scene_exchange(x):
    heads = lax.axis_size("head")
    groups = [
        [
            ((y * SIDE + z) * SIDE + c) * heads + h
            for z in range(SIDE)
            for h in range(heads)
        ]
        for y in range(SIDE)
        for c in range(SIDE)
    ]
    return lax.all_to_all(
        x, ("seq", "head"), split_axis=0, concat_axis=0, axis_index_groups=groups, tiled=True
    )


def gather_axis(x, stride):
    pieces = [x]
    for s in range(1, SIDE):
        pieces.append(ring_shift(x, stride, s))
    return pieces


def scatter_axis(x, stride):
    rows = x.shape[1] // SIDE
    kind = BF16 if stride == 1 else F32
    total = x[:, :rows]
    for s in range(1, SIDE):
        piece = x[:, s * rows : (s + 1) * rows].astype(kind)
        piece = ring_shift(piece, stride, SIDE - s)
        total = total + piece.astype(F32)
    return total


def exchange(x):
    return lax.all_to_all(x, "seq", split_axis=0, concat_axis=0, tiled=True)


def nt(a, b):
    return lax.dot_general(a, b, (((1,), (1,)), ((), ())), preferred_element_type=F32)


def nn(a, b):
    return lax.dot_general(a, b, (((1,), (0,)), ((), ())), preferred_element_type=F32)


def tn(a, b):
    return lax.dot_general(a, b, (((0,), (0,)), ((), ())), preferred_element_type=F32)


def holder_row(token, blocks):
    return (token % BLK) // TAKE * (TAKE * blocks) + token // BLK * TAKE + token % TAKE


def spread_kernel(k, v, out):
    tokens = k.shape[0]
    r = lax.broadcasted_iota(jnp.int32, (tokens, tokens), 0)
    t = lax.broadcasted_iota(jnp.int32, (tokens, tokens), 1)
    order = (holder_row(t, tokens // BLK) == r).astype(F32).astype(BF16)
    out[:tokens] = nn(order, k[...]).astype(BF16)
    out[tokens:] = nn(order, v[...]).astype(BF16)


def spread(k, v):
    tokens, features = k.shape
    width = 2 * DH
    return pl.pallas_call(
        spread_kernel,
        grid=(features // width,),
        in_specs=[pl.BlockSpec((tokens, width), lambda i: (0, i))] * 2,
        out_specs=pl.BlockSpec((2 * tokens, width), lambda i: (0, i)),
        out_shape=jax.ShapeDtypeStruct((2 * tokens, features), BF16),
        name="spread",
    )(k, v)


def plan_kernel(place, counts, pattern, bias, live, live_col, choose):
    rows, tokens = bias.shape
    blocks = tokens // BLK
    total = counts.shape[0]
    position = place[0]
    first = position * blocks
    requests = blocks * RAND
    asked = requests * TAKE

    query_block = lax.broadcasted_iota(jnp.int32, (BLK, tokens), 1) // BLK
    offset = lax.broadcasted_iota(jnp.int32, (BLK, tokens), 0)
    for w in range(blocks + 2):
        block = first + (w - 1)
        count = counts[jnp.minimum(jnp.maximum(block, 0), total - 1)]
        count = jnp.where((block >= 0) & (block < total), count, 0)
        ok = (offset < count) & (query_block <= w) & (query_block + 2 >= w)
        bias[w * BLK : (w + 1) * BLK] = jnp.where(ok, 0.0, -1e30).astype(F32)
    near = (blocks + 2) * BLK
    r = lax.broadcasted_iota(jnp.int32, (asked, tokens), 0)
    column_block = lax.broadcasted_iota(jnp.int32, (asked, tokens), 1) // BLK
    count = jnp.zeros((asked, tokens), jnp.int32)
    for i in range(requests):
        here = (r // TAKE == i) & (column_block == i // RAND)
        count = jnp.where(here, counts[pattern[first + i // RAND, i % RAND]], count)
    for g in range(HOLD):
        ok = r % TAKE + g * TAKE < count
        start = near + g * asked
        bias[start : start + asked] = jnp.where(ok, 0.0, -1e30).astype(F32)
    near = near + HOLD * asked
    bias[near:] = jnp.zeros((rows - near, tokens), F32)

    lane = lax.broadcasted_iota(jnp.int32, (8, tokens), 1)
    bound = jnp.zeros((8, tokens), jnp.int32)
    row = lax.broadcasted_iota(jnp.int32, (BLK, DH), 0)
    for b in range(blocks):
        bound = jnp.where(lane // BLK == b, counts[first + b], bound)
        live_col[b * BLK : (b + 1) * BLK] = (row < counts[first + b]).astype(F32)
    live[...] = (lane % BLK < bound).astype(F32)

    r = lax.broadcasted_iota(jnp.int32, (asked, 128), 0)
    lane = lax.broadcasted_iota(jnp.int32, (asked, 128), 1)
    for d in range(total // blocks):
        start = d * blocks
        take = r % TAKE
        for i in range(requests):
            base = pattern[start + i // RAND, i % RAND] * TAKE
            take = jnp.where(r // TAKE == i, base + r % TAKE, take)
        for w in range(0, choose.shape[1], 128):
            hit = (take == lane + w).astype(F32).astype(BF16)
            choose[d * asked : (d + 1) * asked, w : w + 128] = hit


def plan(place, counts, pattern, tokens, scene_rows):
    smem = pl.BlockSpec(memory_space=pltpu.SMEM)
    blocks = tokens // BLK
    asked = blocks * RAND * TAKE
    rows = (blocks + 2) * BLK + HOLD * asked + scene_rows
    return pl.pallas_call(
        plan_kernel,
        in_specs=[smem, smem, smem],
        out_shape=[
            jax.ShapeDtypeStruct((rows, tokens), F32),
            jax.ShapeDtypeStruct((8, tokens), F32),
            jax.ShapeDtypeStruct((tokens, DH), F32),
            jax.ShapeDtypeStruct((2 * HOLD * asked, counts.shape[0] * TAKE), BF16),
        ],
        name="plan",
    )(place, counts, pattern)


def scores(key, query, bias):
    return nt(key, query) * (DH ** (-0.5) * LOG2E) + bias


def masked_grad(live_col, go):
    return jnp.where(live_col[...] > 0.0, go[...], jnp.zeros((), BF16))


def near_kernel(bias, live_col, q, go, k, v, lo, hi, stats):
    key = jnp.concatenate([lo[0], k[...], hi[0]], axis=0)
    val = jnp.concatenate([lo[1], v[...], hi[1]], axis=0)
    s = scores(key, q[...], bias[: key.shape[0]])
    m = jnp.max(s, axis=0, keepdims=True)
    e = jnp.exp2(s - m)
    stats[0, 0:1] = m
    stats[0, 1:2] = jnp.sum(e, axis=0, keepdims=True)
    dp = nt(val, masked_grad(live_col, go))
    stats[0, 2:3] = jnp.sum(e * dp, axis=0, keepdims=True)


def far_kernel(bias, live_col, q, go, near, rnd, *refs):
    scn_k, scn_v, (d_rnd, d_scn, stats) = refs[:SIDE], refs[SIDE : 2 * SIDE], refs[2 * SIDE :]
    scale = DH ** (-0.5)
    far = rnd.shape[1]
    key = jnp.concatenate([rnd[0]] + [x[...] for x in scn_k], axis=0)
    val = jnp.concatenate([rnd[1]] + [x[...] for x in scn_v], axis=0)
    query = q[...]
    grad = masked_grad(live_col, go)
    s = scores(key, query, bias[bias.shape[0] - key.shape[0] :])
    m = jnp.maximum(near[0, 0:1], jnp.max(s, axis=0, keepdims=True))
    e = jnp.exp2(s - m)
    shrink = jnp.exp2(near[0, 0:1] - m)
    inverse = 1.0 / (near[0, 1:2] * shrink + jnp.sum(e, axis=0, keepdims=True))
    dp = nt(val, grad)
    delta = (near[0, 2:3] * shrink + jnp.sum(e * dp, axis=0, keepdims=True)) * inverse
    stats[0, 0:1] = m
    stats[0, 1:2] = inverse
    stats[0, 2:3] = delta
    p = e * inverse
    d = nn(p.astype(BF16), grad)
    d_rnd[1] = d[:far].astype(BF16)
    d_scn[1] = d[far:]
    d = nn((p * (dp - delta) * scale).astype(BF16), query)
    d_rnd[0] = d[:far].astype(BF16)
    d_scn[0] = d[far:]


def rest_kernel(bias, live, live_col, q, go, stats, k, v, lo, hi, rnd, *refs):
    scn_k, scn_v = refs[:SIDE], refs[SIDE : 2 * SIDE]
    att, dq, d_own, d_halo = refs[2 * SIDE :]
    tokens = q.shape[0]
    window = tokens + 2 * BLK
    scale = DH ** (-0.5)
    key = jnp.concatenate([lo[0], k[...], hi[0], rnd[0]] + [x[...] for x in scn_k], axis=0)
    val = jnp.concatenate([lo[1], v[...], hi[1], rnd[1]] + [x[...] for x in scn_v], axis=0)
    query = q[...]
    grad = masked_grad(live_col, go)
    p = jnp.exp2(scores(key, query, bias[...]) - stats[0, 0:1]) * stats[0, 1:2]
    pb = p.astype(BF16)
    ds = (p * (nt(val, grad) - stats[0, 2:3]) * scale).astype(BF16)
    att[...] = (tn(val, pb) * live[:1]).T.astype(BF16)
    dq[...] = tn(key, ds).T.astype(BF16)
    for which, (left, right) in enumerate(((ds, query), (pb, grad))):
        d = nn(left[:window], right)
        d_halo[which, :BLK] = d[:BLK].astype(BF16)
        d_own[which] = d[BLK : BLK + tokens]
        d_halo[which, BLK:] = d[BLK + tokens :].astype(BF16)


def in_hbm(x):
    return pltpu.with_memory_space_constraint(x, pltpu.HBM)


def whole(x):
    return pl.BlockSpec(x.shape, lambda h: (0,) * x.ndim)


def flat(rows, start=0):
    return pl.BlockSpec((rows, DH), lambda h: (0, h + start))


def pair(rows):
    return pl.BlockSpec((2, rows, DH), lambda h: (0, 0, h))


def per_head(tokens):
    return pl.BlockSpec((1, 8, tokens), lambda h: (h, 0, 0))


def shaped(shape, dtype):
    return jax.ShapeDtypeStruct(shape, dtype)


def kernel_call(kernel, heads, args, in_specs, out_specs, out_shape):
    return pl.pallas_call(
        kernel,
        grid=(heads,),
        in_specs=in_specs,
        out_specs=out_specs,
        out_shape=out_shape,
        compiler_params=pltpu.CompilerParams(vmem_limit_bytes=48 << 20),
    )(*args)


def near_part(bias, live_col, q, go, k, v, lo, hi):
    tokens, features = q.shape
    heads = features // DH
    return kernel_call(
        near_kernel,
        heads,
        (bias, live_col, q, go, k, v, lo, hi),
        [whole(bias), whole(live_col)] + [flat(tokens)] * 4 + [pair(BLK)] * 2,
        per_head(tokens),
        shaped((heads, 8, tokens), F32),
    )


def far_part(bias, live_col, q, go, near, rnd, scn):
    tokens, features = q.shape
    heads = features // DH
    far = rnd.shape[1]
    rows = scn[0].shape[0]
    return kernel_call(
        far_kernel,
        heads,
        (bias, live_col, q, go, near, rnd, *scn, *scn),
        [whole(bias), whole(live_col)]
        + [flat(tokens)] * 2
        + [per_head(tokens), pair(far)]
        + [flat(rows)] * SIDE
        + [flat(rows, heads)] * SIDE,
        [pair(far), pair(SIDE * rows), per_head(tokens)],
        [
            shaped((2, far, features), BF16),
            shaped((2, SIDE * rows, features), F32),
            shaped((heads, 8, tokens), F32),
        ],
    )


def rest_part(bias, live, live_col, q, go, stats, k, v, lo, hi, rnd, scn):
    tokens, features = q.shape
    heads = features // DH
    rows = scn[0].shape[0]
    return kernel_call(
        rest_kernel,
        heads,
        (bias, live, live_col, q, go, stats, k, v, lo, hi, rnd, *scn, *scn),
        [whole(bias), whole(live), whole(live_col)]
        + [flat(tokens)] * 2
        + [per_head(tokens)]
        + [flat(tokens)] * 2
        + [pair(BLK), pair(BLK), pair(rnd.shape[1])]
        + [flat(rows)] * SIDE
        + [flat(rows, heads)] * SIDE,
        [flat(tokens), flat(tokens), pair(tokens), pair(2 * BLK)],
        [
            shaped((tokens, features), BF16),
            shaped((tokens, features), BF16),
            shaped((2, tokens, features), F32),
            shaped((2, 2 * BLK, features), BF16),
        ],
    )


def final_kernel(own, back, left, right, *outs):
    tokens = own.shape[1]
    t = lax.broadcasted_iota(jnp.int32, (tokens, tokens), 0)
    c = lax.broadcasted_iota(jnp.int32, (tokens, tokens), 1)
    order = (holder_row(t, tokens // BLK) == c).astype(F32).astype(BF16)
    for which, out in enumerate(outs):
        total = own[which] + nn(order, back[which * tokens : (which + 1) * tokens])
        edge = jnp.zeros((tokens - BLK, total.shape[1]), F32)
        total = total + jnp.concatenate([left[which].astype(F32), edge], axis=0)
        total = total + jnp.concatenate([edge, right[which].astype(F32)], axis=0)
        out[...] = total.astype(BF16)


def final(own, back, left, right):
    _, tokens, features = own.shape
    width = 2 * DH

    def two(rows):
        return pl.BlockSpec((2, rows, width), lambda i: (0, 0, i))

    def one(rows):
        return pl.BlockSpec((rows, width), lambda i: (0, i))

    return pl.pallas_call(
        final_kernel,
        grid=(features // width,),
        in_specs=[two(tokens), one(back.shape[0]), two(BLK), two(BLK)],
        out_specs=[one(tokens)] * 2,
        out_shape=[jax.ShapeDtypeStruct((tokens, features), BF16)] * 2,
        name="final",
    )(own, back, left, right)


def program(queries, keys, values, grad_out, scene_keys, scene_values, valid, pattern):
    seq = lax.axis_size("seq")
    groups = lax.axis_size("head")
    group = lax.axis_index("head")
    position = lax.axis_index("seq")
    tokens, features = queries.shape
    blocks = tokens // BLK
    asked = blocks * RAND * TAKE
    axes = (SIDE, SIDE * SIDE, 1)

    out_1 = spread(keys, values)
    in_1 = exchange(out_1.reshape(seq, blocks * TAKE, features))

    both = [x.reshape(groups, features) for x in (scene_keys, scene_values)]
    scn = []
    for s in range(groups):
        to = (group + s) % groups
        row = jnp.concatenate([lax.dynamic_slice_in_dim(x, to, 1, 0) for x in both], axis=1)
        scn.append(head_shift(row, s) if s else row)
    scn = jnp.concatenate(scn, axis=0)
    for stride in axes:
        pieces = gather_axis(scn, stride)
        scn = jnp.concatenate(pieces, axis=0) if stride != axes[-1] else pieces
    lo = jnp.stack([keys[tokens - BLK :], values[tokens - BLK :]])
    hi = jnp.stack([keys[:BLK], values[:BLK]])
    lo = passed_along(lo, 1)
    hi = passed_along(hi, -1)

    bias, live, live_col, pick = plan(
        position.reshape(1), valid, pattern, tokens, seq * groups
    )
    out_2 = jnp.einsum(
        "rc,cf->rf", pick, in_1.reshape(-1, features), preferred_element_type=F32
    ).astype(BF16)
    rnd = exchange(out_2.reshape(seq, asked, features)).reshape(2, -1, features)

    near = near_part(bias, live_col, queries, grad_out, keys, values, lo, hi)
    near, *scn = (in_hbm(x) for x in (near, *scn))
    d_rnd, d_scn, stats = far_part(bias, live_col, queries, grad_out, near, rnd, scn)

    back_1 = exchange(d_rnd.reshape(seq, asked, features))
    attended, grad_query, d_own, d_halo = rest_part(
        bias, live, live_col, queries, grad_out, stats, keys, values, lo, hi, rnd, scn
    )
    from_right = passed_along(d_halo[:, :BLK], -1)
    from_left = passed_along(d_halo[:, BLK:], 1)
    for stride in (1, SIDE * SIDE):
        d_scn = scatter_axis(d_scn, stride)
    d_scn = jnp.concatenate([d_scn[0], d_scn[1]], axis=1).astype(BF16)
    j = jnp.arange(SIDE * groups, dtype=jnp.int32)
    near_z = (position // SIDE - j // groups) % SIDE
    lies_at = near_z * groups + (group - j % groups) % groups
    by_owner = (lies_at[:, None] == j[None, :]).astype(BF16)
    d_scn = jnp.einsum("rs,sf->rf", by_owner, d_scn, preferred_element_type=F32).astype(BF16)
    d_scn = scene_exchange(d_scn)
    d_scn = jnp.sum(d_scn.reshape(SIDE, groups, 2 * features).astype(F32), axis=0).astype(BF16)
    totals = [
        d_scn[:, which * features : (which + 1) * features].reshape(1, groups * features)
        for which in range(2)
    ]

    held = jnp.einsum(
        "rc,rf->cf", pick, back_1.reshape(-1, features), preferred_element_type=F32
    ).astype(BF16)
    back_2 = exchange(held.reshape(seq, blocks * TAKE, features))
    grads = final(d_own, back_2.reshape(-1, features), from_left, from_right)
    return (attended, grad_query, grads[0], grads[1], totals[0], totals[1])


def solution(mesh):
    block = P("seq", "head")
    rows = P(("seq", "head"), None)
    return jax.shard_map(
        program,
        mesh=mesh,
        in_specs=(block, block, block, block, rows, rows, P(), P()),
        out_specs=(block, block, block, block, rows, rows),
        check_vma=False,
    )
```

```python
import jax
import jax.numpy as jnp
from jax import lax
from jax.experimental import pallas as pl
from jax.experimental.pallas import tpu as pltpu
from jax.sharding import PartitionSpec as P


DH = 128
BLK = 64
RAND = 3
SIDE = 4
HOLD = 32
TAKE = BLK // HOLD
F32 = jnp.float32
BF16 = jnp.bfloat16
LOG2E = 1.4426950408889634


def ring_shift(x, stride, by):
    pairs = []
    for i in range(lax.axis_size("seq")):
        c = i // stride % SIDE
        pairs.append((i, i + ((c + by) % SIDE - c) * stride))
    return lax.ppermute(x, "seq", pairs)


def passed_along(x, by):
    length = lax.axis_size("seq")
    pairs = [(i, i + by) for i in range(length) if 0 <= i + by < length]
    return lax.ppermute(x, "seq", pairs)


def head_shift(x, by):
    count = lax.axis_size("head")
    return lax.ppermute(x, "head", [(i, (i + by) % count) for i in range(count)])


def gather_axis(x, stride):
    pieces = [x]
    for s in range(1, SIDE):
        pieces.append(ring_shift(x, stride, s))
    return pieces


def scatter_axis(x, stride):
    rows = x.shape[1] // SIDE
    kind = BF16 if stride == 1 else F32
    total = x[:, :rows]
    for s in range(1, SIDE):
        piece = x[:, s * rows : (s + 1) * rows].astype(kind)
        piece = ring_shift(piece, stride, SIDE - s)
        total = total + piece.astype(F32)
    return total


def exchange(x):
    return lax.all_to_all(x, "seq", split_axis=0, concat_axis=0, tiled=True)


def nt(a, b):
    return lax.dot_general(a, b, (((1,), (1,)), ((), ())), preferred_element_type=F32)


def nn(a, b):
    return lax.dot_general(a, b, (((1,), (0,)), ((), ())), preferred_element_type=F32)


def tn(a, b):
    return lax.dot_general(a, b, (((0,), (0,)), ((), ())), preferred_element_type=F32)


def holder_row(token, blocks):
    return (token % BLK) // TAKE * (TAKE * blocks) + token // BLK * TAKE + token % TAKE


def spread_kernel(k, v, out):
    tokens = k.shape[0]
    r = lax.broadcasted_iota(jnp.int32, (tokens, tokens), 0)
    t = lax.broadcasted_iota(jnp.int32, (tokens, tokens), 1)
    order = (holder_row(t, tokens // BLK) == r).astype(F32).astype(BF16)
    out[:tokens] = nn(order, k[...]).astype(BF16)
    out[tokens:] = nn(order, v[...]).astype(BF16)


def spread(k, v):
    tokens, features = k.shape
    width = 2 * DH
    return pl.pallas_call(
        spread_kernel,
        grid=(features // width,),
        in_specs=[pl.BlockSpec((tokens, width), lambda i: (0, i))] * 2,
        out_specs=pl.BlockSpec((2 * tokens, width), lambda i: (0, i)),
        out_shape=jax.ShapeDtypeStruct((2 * tokens, features), BF16),
        name="spread",
    )(k, v)


def plan_kernel(place, counts, pattern, bias, live, live_col, choose):
    rows, tokens = bias.shape
    blocks = tokens // BLK
    total = counts.shape[0]
    position = place[0]
    first = position * blocks
    requests = blocks * RAND
    asked = requests * TAKE

    query_block = lax.broadcasted_iota(jnp.int32, (BLK, tokens), 1) // BLK
    offset = lax.broadcasted_iota(jnp.int32, (BLK, tokens), 0)
    for w in range(blocks + 2):
        block = first + (w - 1)
        count = counts[jnp.minimum(jnp.maximum(block, 0), total - 1)]
        count = jnp.where((block >= 0) & (block < total), count, 0)
        ok = (offset < count) & (query_block <= w) & (query_block + 2 >= w)
        bias[w * BLK : (w + 1) * BLK] = jnp.where(ok, 0.0, -1e30).astype(F32)
    near = (blocks + 2) * BLK
    r = lax.broadcasted_iota(jnp.int32, (asked, tokens), 0)
    column_block = lax.broadcasted_iota(jnp.int32, (asked, tokens), 1) // BLK
    count = jnp.zeros((asked, tokens), jnp.int32)
    for i in range(requests):
        here = (r // TAKE == i) & (column_block == i // RAND)
        count = jnp.where(here, counts[pattern[first + i // RAND, i % RAND]], count)
    for g in range(HOLD):
        ok = r % TAKE + g * TAKE < count
        start = near + g * asked
        bias[start : start + asked] = jnp.where(ok, 0.0, -1e30).astype(F32)
    near = near + HOLD * asked
    bias[near:] = jnp.zeros((rows - near, tokens), F32)

    lane = lax.broadcasted_iota(jnp.int32, (8, tokens), 1)
    bound = jnp.zeros((8, tokens), jnp.int32)
    row = lax.broadcasted_iota(jnp.int32, (BLK, DH), 0)
    for b in range(blocks):
        bound = jnp.where(lane // BLK == b, counts[first + b], bound)
        live_col[b * BLK : (b + 1) * BLK] = (row < counts[first + b]).astype(F32)
    live[...] = (lane % BLK < bound).astype(F32)

    r = lax.broadcasted_iota(jnp.int32, (asked, 128), 0)
    lane = lax.broadcasted_iota(jnp.int32, (asked, 128), 1)
    for d in range(total // blocks):
        start = d * blocks
        take = r % TAKE
        for i in range(requests):
            base = pattern[start + i // RAND, i % RAND] * TAKE
            take = jnp.where(r // TAKE == i, base + r % TAKE, take)
        for w in range(0, choose.shape[1], 128):
            hit = (take == lane + w).astype(F32).astype(BF16)
            choose[d * asked : (d + 1) * asked, w : w + 128] = hit


def plan(place, counts, pattern, tokens, scene_rows):
    smem = pl.BlockSpec(memory_space=pltpu.SMEM)
    blocks = tokens // BLK
    asked = blocks * RAND * TAKE
    rows = (blocks + 2) * BLK + HOLD * asked + scene_rows
    return pl.pallas_call(
        plan_kernel,
        in_specs=[smem, smem, smem],
        out_shape=[
            jax.ShapeDtypeStruct((rows, tokens), F32),
            jax.ShapeDtypeStruct((8, tokens), F32),
            jax.ShapeDtypeStruct((tokens, DH), F32),
            jax.ShapeDtypeStruct((2 * HOLD * asked, counts.shape[0] * TAKE), BF16),
        ],
        name="plan",
    )(place, counts, pattern)


def scores(key, query, bias):
    return nt(key, query) * (DH ** (-0.5) * LOG2E) + bias


def masked_grad(live_col, go):
    return jnp.where(live_col[...] > 0.0, go[...], jnp.zeros((), BF16))


def near_kernel(bias, live_col, q, go, k, v, lo, hi, stats):
    key = jnp.concatenate([lo[0], k[...], hi[0]], axis=0)
    val = jnp.concatenate([lo[1], v[...], hi[1]], axis=0)
    s = scores(key, q[...], bias[: key.shape[0]])
    m = jnp.max(s, axis=0, keepdims=True)
    e = jnp.exp2(s - m)
    stats[0, 0:1] = m
    stats[0, 1:2] = jnp.sum(e, axis=0, keepdims=True)
    dp = nt(val, masked_grad(live_col, go))
    stats[0, 2:3] = jnp.sum(e * dp, axis=0, keepdims=True)


def far_kernel(bias, live_col, q, go, near, rnd, *refs):
    scn_k, scn_v, (d_rnd, d_scn, stats) = refs[:SIDE], refs[SIDE : 2 * SIDE], refs[2 * SIDE :]
    scale = DH ** (-0.5)
    far = rnd.shape[1]
    key = jnp.concatenate([rnd[0]] + [x[...] for x in scn_k], axis=0)
    val = jnp.concatenate([rnd[1]] + [x[...] for x in scn_v], axis=0)
    query = q[...]
    grad = masked_grad(live_col, go)
    s = scores(key, query, bias[bias.shape[0] - key.shape[0] :])
    m = jnp.maximum(near[0, 0:1], jnp.max(s, axis=0, keepdims=True))
    e = jnp.exp2(s - m)
    shrink = jnp.exp2(near[0, 0:1] - m)
    inverse = 1.0 / (near[0, 1:2] * shrink + jnp.sum(e, axis=0, keepdims=True))
    dp = nt(val, grad)
    delta = (near[0, 2:3] * shrink + jnp.sum(e * dp, axis=0, keepdims=True)) * inverse
    stats[0, 0:1] = m
    stats[0, 1:2] = inverse
    stats[0, 2:3] = delta
    p = e * inverse
    d = nn(p.astype(BF16), grad)
    d_rnd[1] = d[:far].astype(BF16)
    d_scn[1] = d[far:]
    d = nn((p * (dp - delta) * scale).astype(BF16), query)
    d_rnd[0] = d[:far].astype(BF16)
    d_scn[0] = d[far:]


def rest_kernel(bias, live, live_col, q, go, stats, k, v, lo, hi, rnd, *refs):
    scn_k, scn_v = refs[:SIDE], refs[SIDE : 2 * SIDE]
    att, dq, d_own, d_halo = refs[2 * SIDE :]
    tokens = q.shape[0]
    window = tokens + 2 * BLK
    scale = DH ** (-0.5)
    key = jnp.concatenate([lo[0], k[...], hi[0], rnd[0]] + [x[...] for x in scn_k], axis=0)
    val = jnp.concatenate([lo[1], v[...], hi[1], rnd[1]] + [x[...] for x in scn_v], axis=0)
    query = q[...]
    grad = masked_grad(live_col, go)
    p = jnp.exp2(scores(key, query, bias[...]) - stats[0, 0:1]) * stats[0, 1:2]
    pb = p.astype(BF16)
    ds = (p * (nt(val, grad) - stats[0, 2:3]) * scale).astype(BF16)
    att[...] = (tn(val, pb) * live[:1]).T.astype(BF16)
    dq[...] = tn(key, ds).T.astype(BF16)
    for which, (left, right) in enumerate(((ds, query), (pb, grad))):
        d = nn(left[:window], right)
        d_halo[which, :BLK] = d[:BLK].astype(BF16)
        d_own[which] = d[BLK : BLK + tokens]
        d_halo[which, BLK:] = d[BLK + tokens :].astype(BF16)


def in_hbm(x):
    return pltpu.with_memory_space_constraint(x, pltpu.HBM)


def whole(x):
    return pl.BlockSpec(x.shape, lambda h: (0,) * x.ndim)


def flat(rows, start=0):
    return pl.BlockSpec((rows, DH), lambda h: (0, h + start))


def pair(rows):
    return pl.BlockSpec((2, rows, DH), lambda h: (0, 0, h))


def per_head(tokens):
    return pl.BlockSpec((1, 8, tokens), lambda h: (h, 0, 0))


def shaped(shape, dtype):
    return jax.ShapeDtypeStruct(shape, dtype)


def kernel_call(kernel, heads, args, in_specs, out_specs, out_shape):
    return pl.pallas_call(
        kernel,
        grid=(heads,),
        in_specs=in_specs,
        out_specs=out_specs,
        out_shape=out_shape,
        compiler_params=pltpu.CompilerParams(vmem_limit_bytes=48 << 20),
    )(*args)


def near_part(bias, live_col, q, go, k, v, lo, hi):
    tokens, features = q.shape
    heads = features // DH
    return kernel_call(
        near_kernel,
        heads,
        (bias, live_col, q, go, k, v, lo, hi),
        [whole(bias), whole(live_col)] + [flat(tokens)] * 4 + [pair(BLK)] * 2,
        per_head(tokens),
        shaped((heads, 8, tokens), F32),
    )


def far_part(bias, live_col, q, go, near, rnd, scn):
    tokens, features = q.shape
    heads = features // DH
    far = rnd.shape[1]
    rows = scn[0].shape[0]
    return kernel_call(
        far_kernel,
        heads,
        (bias, live_col, q, go, near, rnd, *scn, *scn),
        [whole(bias), whole(live_col)]
        + [flat(tokens)] * 2
        + [per_head(tokens), pair(far)]
        + [flat(rows)] * SIDE
        + [flat(rows, heads)] * SIDE,
        [pair(far), pair(SIDE * rows), per_head(tokens)],
        [
            shaped((2, far, features), BF16),
            shaped((2, SIDE * rows, features), F32),
            shaped((heads, 8, tokens), F32),
        ],
    )


def rest_part(bias, live, live_col, q, go, stats, k, v, lo, hi, rnd, scn):
    tokens, features = q.shape
    heads = features // DH
    rows = scn[0].shape[0]
    return kernel_call(
        rest_kernel,
        heads,
        (bias, live, live_col, q, go, stats, k, v, lo, hi, rnd, *scn, *scn),
        [whole(bias), whole(live), whole(live_col)]
        + [flat(tokens)] * 2
        + [per_head(tokens)]
        + [flat(tokens)] * 2
        + [pair(BLK), pair(BLK), pair(rnd.shape[1])]
        + [flat(rows)] * SIDE
        + [flat(rows, heads)] * SIDE,
        [flat(tokens), flat(tokens), pair(tokens), pair(2 * BLK)],
        [
            shaped((tokens, features), BF16),
            shaped((tokens, features), BF16),
            shaped((2, tokens, features), F32),
            shaped((2, 2 * BLK, features), BF16),
        ],
    )


def final_kernel(own, back, left, right, *outs):
    tokens = own.shape[1]
    t = lax.broadcasted_iota(jnp.int32, (tokens, tokens), 0)
    c = lax.broadcasted_iota(jnp.int32, (tokens, tokens), 1)
    order = (holder_row(t, tokens // BLK) == c).astype(F32).astype(BF16)
    for which, out in enumerate(outs):
        total = own[which] + nn(order, back[which * tokens : (which + 1) * tokens])
        edge = jnp.zeros((tokens - BLK, total.shape[1]), F32)
        total = total + jnp.concatenate([left[which].astype(F32), edge], axis=0)
        total = total + jnp.concatenate([edge, right[which].astype(F32)], axis=0)
        out[...] = total.astype(BF16)


def final(own, back, left, right):
    _, tokens, features = own.shape
    width = 2 * DH

    def two(rows):
        return pl.BlockSpec((2, rows, width), lambda i: (0, 0, i))

    def one(rows):
        return pl.BlockSpec((rows, width), lambda i: (0, i))

    return pl.pallas_call(
        final_kernel,
        grid=(features // width,),
        in_specs=[two(tokens), one(back.shape[0]), two(BLK), two(BLK)],
        out_specs=[one(tokens)] * 2,
        out_shape=[jax.ShapeDtypeStruct((tokens, features), BF16)] * 2,
        name="final",
    )(own, back, left, right)


def program(queries, keys, values, grad_out, scene_keys, scene_values, valid, pattern):
    seq = lax.axis_size("seq")
    groups = lax.axis_size("head")
    group = lax.axis_index("head")
    position = lax.axis_index("seq")
    tokens, features = queries.shape
    blocks = tokens // BLK
    asked = blocks * RAND * TAKE
    axes = (SIDE, SIDE * SIDE, 1)

    out_1 = spread(keys, values)
    in_1 = exchange(out_1.reshape(seq, blocks * TAKE, features))

    both = [x.reshape(groups, features) for x in (scene_keys, scene_values)]
    scn = []
    for s in range(groups):
        to = (group + s) % groups
        row = jnp.concatenate([lax.dynamic_slice_in_dim(x, to, 1, 0) for x in both], axis=1)
        scn.append(head_shift(row, s) if s else row)
    scn = jnp.concatenate(scn, axis=0)
    for stride in axes:
        pieces = gather_axis(scn, stride)
        scn = jnp.concatenate(pieces, axis=0) if stride != axes[-1] else pieces
    lo = jnp.stack([keys[tokens - BLK :], values[tokens - BLK :]])
    hi = jnp.stack([keys[:BLK], values[:BLK]])
    lo = passed_along(lo, 1)
    hi = passed_along(hi, -1)

    bias, live, live_col, pick = plan(
        position.reshape(1), valid, pattern, tokens, seq * groups
    )
    out_2 = jnp.einsum(
        "rc,cf->rf", pick, in_1.reshape(-1, features), preferred_element_type=F32
    ).astype(BF16)
    rnd = exchange(out_2.reshape(seq, asked, features)).reshape(2, -1, features)

    near = near_part(bias, live_col, queries, grad_out, keys, values, lo, hi)
    near = in_hbm(near)
    scn = [scn[0]] + [in_hbm(x) for x in scn[1:]]
    d_rnd, d_scn, stats = far_part(bias, live_col, queries, grad_out, near, rnd, scn)

    back_1 = exchange(d_rnd.reshape(seq, asked, features))
    attended, grad_query, d_own, d_halo = rest_part(
        bias, live, live_col, queries, grad_out, stats, keys, values, lo, hi, rnd, scn
    )
    from_right = passed_along(d_halo[:, :BLK], -1)
    from_left = passed_along(d_halo[:, BLK:], 1)
    for stride in reversed(axes):
        d_scn = scatter_axis(d_scn, stride)
    d_scn = jnp.concatenate([d_scn[0], d_scn[1]], axis=1).astype(BF16)
    totals = [jnp.zeros((groups, features), BF16)] * 2
    for s in range(groups):
        row = d_scn[s : s + 1]
        row = head_shift(row, groups - s) if s else row
        at = (group + s) % groups
        for which in range(2):
            totals[which] = lax.dynamic_update_slice_in_dim(
                totals[which], row[:, which * features : (which + 1) * features], at, 0
            )
    totals = [x.reshape(1, groups * features) for x in totals]

    held = jnp.einsum(
        "rc,rf->cf", pick, back_1.reshape(-1, features), preferred_element_type=F32
    ).astype(BF16)
    back_2 = exchange(held.reshape(seq, blocks * TAKE, features))
    grads = final(d_own, back_2.reshape(-1, features), from_left, from_right)
    return (attended, grad_query, grads[0], grads[1], totals[0], totals[1])


def solution(mesh):
    block = P("seq", "head")
    rows = P(("seq", "head"), None)
    return jax.shard_map(
        program,
        mesh=mesh,
        in_specs=(block, block, block, block, rows, rows, P(), P()),
        out_specs=(block, block, block, block, rows, rows),
        check_vma=False,
    )
```
